32 devices in a mesh: fsdp: 16 (over z, y, core), tp: 2 (over x).
Axes of the slice: x: 2, y: 2, z: 4, core: 2. Of those that a mesh axis runs over, the one named last changes fastest.
Arguments:
- tokens: bfloat16 [9472, 768], P(('fsdp', 'tp')), may hold values from -6 to 6
- qkv_weight: bfloat16 [2, 768, 3, 768], P(None, 'fsdp', None, 'tp'), may hold values from -0.21875 to 0.21875
- out_weight: bfloat16 [2, 768, 768], P(None, 'tp', 'fsdp'), may hold values from -1.75 to 1.75
- up_weight: bfloat16 [2, 768, 3072], P(None, 'fsdp', 'tp'), may hold values from -0.21875 to 0.21875
- down_weight: bfloat16 [2, 3072, 768], P(None, 'tp', 'fsdp'), may hold values from -0.109375 to 0.109375
- norm_gain: float32 [2, 2, 768], replicated, may hold values from 0.5 to 1.5
- norm_shift: float32 [2, 2, 768], replicated, may hold values from -1.8 to 1.8
- qv_bias: float32 [2, 2, 768], replicated, may hold values from -1.8 to 1.8
- out_bias: float32 [2, 2, 768], replicated, may hold values from -1.8 to 1.8
- up_bias: float32 [2, 3072], replicated, may hold values from -1.8 to 1.8
- cotangent: bfloat16 [9472, 768], P(('fsdp', 'tp')), may hold values from -6 to 6
Outputs:
- activations: bfloat16 [9472, 768], P(('fsdp', 'tp'))
- input_grad: float32 [9472, 768], P(('fsdp', 'tp'))
- qkv_grad: float32 [2, 768, 3, 768], P(None, 'fsdp', None, 'tp')
- out_grad: float32 [2, 768, 768], P(None, 'tp', 'fsdp')
- up_grad: float32 [2, 768, 3072], P(None, 'fsdp', 'tp')
- down_grad: float32 [2, 3072, 768], P(None, 'tp', 'fsdp')
- gain_grad: float32 [2, 2, 768], replicated
- shift_grad: float32 [2, 2, 768], replicated
- qv_bias_grad: float32 [2, 2, 768], replicated
- out_bias_grad: float32 [2, 2, 768], replicated
- up_bias_grad: float32 [2, 3072], replicated
The draws below stay inside these ranges and needn't reach their ends.
All inputs are finite; a program needn't handle non-finite values.
Results may differ from the reference program's by a relative error of at most 0.017.
Values may be sent and summed in bfloat16 or wider, within the bound.
No kernel may reach another device: no remote copies, remote signals or barrier semaphores. Data moves between devices by JAX's collectives and lax.ppermute only.
A program may use at most 128 MiB of HBM per device.

```python
import jax
import jax.numpy as jnp
from jax import lax

D = 768
HEADS = 12
FF = 3072
SEQ = 197
LAYERS = 2
IMG_DEV = 3
HALF = 296
PADDED = 9472
N_FSDP = 16


def steps_of(key, extent, cuts, low, high):
    level = 1.0
    for axis_at, blocks in cuts:
        steps = jax.random.uniform(jax.random.fold_in(jax.random.fold_in(key, 6), axis_at), (blocks,), jnp.float32, low / len(cuts), high / len(cuts))
        level = level * jnp.repeat(jnp.exp(steps), extent[axis_at] // blocks).reshape((-1,) + (1,) * (len(extent) - 1 - axis_at))
    return level


def gaussian(key, extent, width, reach, split=(), held_as=jnp.bfloat16):
    values = width * jax.random.normal(key, extent, jnp.float32)
    if split:
        values = values * steps_of(key, extent, split, -0.22, 0.18)
    return jnp.clip(values, -reach, reach).astype(held_as)


def setup_inputs(seed: int = 0) -> dict:
    keys = jax.random.split(jax.random.key(seed), 12)
    tokens = gaussian(keys[0], (PADDED, D), 1.0, 6.0, ((0, 32),))
    qkv_weight = gaussian(keys[1], (LAYERS, D, 3, D), D ** -0.5, 0.21875, ((1, 16), (3, 2)))
    out_weight = gaussian(keys[2], (LAYERS, D, D), (D // 64) ** -0.5, 1.75, ((1, 2), (2, 16)))
    up_weight = gaussian(keys[3], (LAYERS, D, FF), D ** -0.5, 0.21875, ((1, 16), (2, 2)))
    down_weight = gaussian(keys[4], (LAYERS, FF, D), FF ** -0.5, 0.109375, ((1, 2), (2, 16)))
    norm_gain = jnp.clip(1.0 + 0.1 * jax.random.normal(keys[5], (LAYERS, 2, D), jnp.float32), 0.5, 1.5)
    norm_shift = gaussian(keys[6], (LAYERS, 2, D), 0.3, 1.8, (), jnp.float32)
    qv_bias = gaussian(keys[7], (LAYERS, 2, D), 0.3, 1.8, (), jnp.float32)
    out_bias = gaussian(keys[8], (LAYERS, 2, D), 0.3, 1.8, (), jnp.float32)
    up_bias = gaussian(keys[9], (LAYERS, FF), 0.3, 1.8, (), jnp.float32)
    cotangent = gaussian(keys[10], (PADDED, D), 1.0, 6.0, ((0, 32),))
    return {"tokens": tokens, "qkv_weight": qkv_weight, "out_weight": out_weight, "up_weight": up_weight, "down_weight": down_weight, "norm_gain": norm_gain, "norm_shift": norm_shift, "qv_bias": qv_bias, "out_bias": out_bias, "up_bias": up_bias, "cotangent": cotangent}


@jax.custom_vjp
def low(v):
    return lax.optimization_barrier(v.astype(jnp.bfloat16)).astype(jnp.float32)

@jax.custom_vjp
def low_back(v):
    return v

def low_keep(v):
    return (low(v), None)

def low_pass(kept, grad):
    return (grad,)

def back_keep(v):
    return (v, None)

def back_low(kept, grad):
    return (low(grad),)
low.defvjp(low_keep, low_pass)
low_back.defvjp(back_keep, back_low)

def exact_einsum(form, left, right):
    return jnp.einsum(form, left, right, precision=lax.Precision.HIGHEST)

def norm_rows(value, gain_vector, shift_vector):
    row_mean = lax.optimization_barrier(jnp.mean(value, axis=-1, keepdims=True))
    centred = value - row_mean
    row_var = lax.optimization_barrier(jnp.mean(centred * centred, axis=-1, keepdims=True))
    return centred * lax.rsqrt(row_var + 1e-06) * gain_vector + shift_vector

def one_layer(group_rows, params):
    qkv_full, out_full, up_full, down_full, gain_pair, shift_pair, qv_pair, out_pair, up_vector = params
    images = group_rows.shape[0]
    head_dim = D // HEADS
    grid_shape = (images, SEQ, HEADS, head_dim)
    hidden = low(norm_rows(group_rows, gain_pair[0], shift_pair[0]))
    projected = exact_einsum('isd,dcn->iscn', hidden, qkv_full)
    queries = low_back(low(projected[:, :, 0] + qv_pair[0])).reshape(grid_shape)
    key_rows = low_back(low(projected[:, :, 1])).reshape(grid_shape)
    values = low_back(low(projected[:, :, 2] + qv_pair[1])).reshape(grid_shape)
    scores = low_back(exact_einsum('ishd,ithd->ihst', queries, key_rows) * head_dim ** (-0.5))
    soft_weights = low(jax.nn.softmax(scores, axis=-1))
    mixed = exact_einsum('ihst,ithd->ishd', soft_weights, values).reshape(images, SEQ, D)
    mixed = low_back(low(mixed))
    branch = low_back(exact_einsum('isd,de->ise', mixed, out_full) + out_pair[0])
    middle = group_rows + branch
    hidden_two = low(norm_rows(middle, gain_pair[1], shift_pair[1]))
    pre_gelu = low_back(exact_einsum('isd,df->isf', hidden_two, up_full) + up_vector)
    activated = low(jax.nn.gelu(pre_gelu, approximate=False))
    branch_two = low_back(exact_einsum('isf,fd->isd', activated, down_full) + out_pair[1])
    return middle + branch_two

def unpad(array):
    grouped = array.astype(jnp.float32).reshape(N_FSDP, 2 * HALF, D)
    return grouped[:, :IMG_DEV * SEQ].reshape(N_FSDP, IMG_DEV, SEQ, D)

def repad(array):
    grouped = array.reshape(N_FSDP, IMG_DEV * SEQ, D)
    filler = jnp.zeros((N_FSDP, 2 * HALF - IMG_DEV * SEQ, D), array.dtype)
    return jnp.concatenate([grouped, filler], axis=1).reshape(N_FSDP * 2 * HALF, D)

def reference(tokens, qkv_weight, out_weight, up_weight, down_weight, norm_gain, norm_shift, qv_bias, out_bias, up_bias, cotangent):
    params = tuple((array.astype(jnp.float32) for array in (qkv_weight, out_weight, up_weight, down_weight, norm_gain, norm_shift, qv_bias, out_bias, up_bias)))
    start_rows = unpad(tokens)

    def forward(start_rows, params):

        def group_pass(group_rows):
            for layer_index in range(LAYERS):
                group_rows = one_layer(group_rows, tuple((param[layer_index] for param in params)))
            return group_rows
        return lax.map(jax.checkpoint(group_pass), start_rows)
    result, pullback = jax.vjp(forward, start_rows, params)
    input_grad, weight_grads = pullback(unpad(cotangent))
    activations = repad(result).astype(jnp.bfloat16)
    return (activations, repad(input_grad), weight_grads[0], weight_grads[1], weight_grads[2], weight_grads[3], weight_grads[4], weight_grads[5], weight_grads[6], weight_grads[7], weight_grads[8])
```

```python
from functools import partial

import jax
import jax.numpy as jnp
from jax import lax
from jax.sharding import PartitionSpec as P

D = 768
HEADS = 12
FF = 3072
SEQ = 197
LAYERS = 2
IMG_DEV = 3


def norm_rows(value, gain_vector, shift_vector):
    row_mean = jnp.mean(value, axis=-1, keepdims=True)
    centred = value - row_mean
    row_var = jnp.mean(centred * centred, axis=-1, keepdims=True)
    return centred * lax.rsqrt(row_var + 1e-06) * gain_vector + shift_vector


def row_product(left, right):
    return lax.dot_general(
        left, right, (((0,), (0,)), ((), ())), preferred_element_type=jnp.float32
    )


def back_product(left, right):
    return lax.dot_general(
        left, right, (((1,), (1,)), ((), ())), preferred_element_type=jnp.float32
    )


def halves(own, other, first):
    return jnp.concatenate(
        [jnp.where(first, own, other), jnp.where(first, other, own)], axis=0
    )


def swap(value):
    return lax.ppermute(value, "tp", [(0, 1), (1, 0)])


def summed_everywhere(value, fsdp_count):
    step = 1
    while step < fsdp_count:
        value = value + lax.ppermute(
            value, "fsdp", [(place, place ^ step) for place in range(fsdp_count)]
        )
        step *= 2
    return value + swap(value)


def gathered(pieces):
    return lax.all_gather(jnp.concatenate(pieces, axis=1), "fsdp", axis=0, tiled=True)


def scattered(pieces):
    joined = jnp.concatenate([piece.astype(jnp.bfloat16) for piece in pieces], axis=1)
    return lax.psum_scatter(joined, "fsdp", scatter_dimension=0, tiled=True).astype(jnp.float32)


def attend(queries, key_rows, values, images, local_heads, head_dim):
    grid_shape = (images, SEQ, local_heads, head_dim)
    scores = jnp.einsum(
        "ishd,ithd->ihst",
        queries.reshape(grid_shape),
        key_rows.reshape(grid_shape),
        preferred_element_type=jnp.float32,
    ) * head_dim ** (-0.5)
    row_max = jnp.max(scores, axis=-1, keepdims=True)
    expanded = jnp.exp(scores - row_max)
    row_total = jnp.sum(expanded, axis=-1, keepdims=True)
    soft_weights = (expanded / row_total).astype(jnp.bfloat16)
    log_total = row_max + jnp.log(row_total)
    mixed = jnp.einsum(
        "ihst,ithd->ishd",
        soft_weights,
        values.reshape(grid_shape),
        preferred_element_type=jnp.float32,
    )
    return (mixed.reshape(images * SEQ, local_heads * head_dim).astype(jnp.bfloat16), log_total)


def attend_back(mixed_grad, queries, key_rows, values, log_total, images, local_heads, head_dim):
    grid_shape = (images, SEQ, local_heads, head_dim)
    query_grid = queries.reshape(grid_shape)
    key_grid = key_rows.reshape(grid_shape)
    value_grid = values.reshape(grid_shape)
    grad_grid = mixed_grad.reshape(grid_shape)
    scale = head_dim ** (-0.5)
    scores = (
        jnp.einsum("ishd,ithd->ihst", query_grid, key_grid, preferred_element_type=jnp.float32)
        * scale
    )
    chances = jnp.exp(scores - log_total)
    soft_weights = chances.astype(jnp.bfloat16)
    value_grad = jnp.einsum(
        "ihst,ishd->ithd", soft_weights, grad_grid, preferred_element_type=jnp.float32
    ).astype(jnp.bfloat16)
    weight_grad = jnp.einsum(
        "ishd,ithd->ihst", grad_grid, value_grid, preferred_element_type=jnp.float32
    )
    score_grad = (
        chances * (weight_grad - jnp.sum(weight_grad * chances, axis=-1, keepdims=True))
    ).astype(jnp.bfloat16)
    query_grad = (
        jnp.einsum("ihst,ithd->ishd", score_grad, key_grid, preferred_element_type=jnp.float32)
        * scale
    ).astype(jnp.bfloat16)
    key_grad = (
        jnp.einsum("ihst,ishd->ithd", score_grad, query_grid, preferred_element_type=jnp.float32)
        * scale
    ).astype(jnp.bfloat16)
    flat_shape = (images * SEQ, local_heads * head_dim)
    return jnp.stack(
        [
            query_grad.reshape(flat_shape),
            key_grad.reshape(flat_shape),
            value_grad.reshape(flat_shape),
        ],
        axis=1,
    )


def on_device(
    tokens,
    qkv_weight,
    out_weight,
    up_weight,
    down_weight,
    norm_gain,
    norm_shift,
    qv_bias,
    out_bias,
    up_bias,
    cotangent,
):
    tp_index = lax.axis_index("tp")
    tp_count = lax.axis_size("tp")
    fsdp_count = lax.axis_size("fsdp")
    row_count = tokens.shape[0]
    local_width = qkv_weight.shape[3]
    inner_width = up_weight.shape[2]
    piece_rows = qkv_weight.shape[1]
    local_heads = HEADS // tp_count
    head_dim = D // HEADS
    images = IMG_DEV
    all_rows = images * SEQ
    slot_rows = row_count * tp_count
    first = tp_index == 0
    live = (tp_index * row_count + jnp.arange(row_count) < all_rows)[:, None]
    cut_qkv = 3 * local_width
    cut_out = cut_qkv + local_width
    cut_up = cut_out + inner_width
    cut_down = cut_up + inner_width

    def padded(value):
        filler = jnp.zeros((slot_rows - all_rows,) + value.shape[1:], value.dtype)
        return jnp.concatenate([value, filler], axis=0)

    def own_rows(value):
        return lax.dynamic_slice_in_dim(value, tp_index * row_count, row_count, 0)

    def other_rows(value):
        return lax.dynamic_slice_in_dim(value, (1 - tp_index) * row_count, row_count, 0)

    def shared_sum(product, own_left, other_left, weight):
        sent = swap(product(other_left, weight).astype(jnp.bfloat16))
        return product(own_left, weight) + sent.astype(jnp.float32)

    def plain(left, right):
        return jnp.dot(left, right, preferred_element_type=jnp.float32)

    def attn_pieces(layer_index):
        return [
            qkv_weight[layer_index].reshape(piece_rows, cut_qkv),
            out_weight[layer_index].T,
        ]

    def mlp_pieces(layer_index):
        return [up_weight[layer_index], down_weight[layer_index].T]

    attn_zero = gathered(attn_pieces(0))
    mlp_zero = gathered(mlp_pieces(0))
    full_one = gathered(attn_pieces(1) + mlp_pieces(1))
    weights = [
        (
            attn_zero[:, :cut_qkv],
            attn_zero[:, cut_qkv:],
            mlp_zero[:, :inner_width],
            mlp_zero[:, inner_width:],
        ),
        (
            full_one[:, :cut_qkv],
            full_one[:, cut_qkv:cut_out],
            full_one[:, cut_out:cut_up],
            full_one[:, cut_up:cut_down],
        ),
    ]

    stream = tokens.astype(jnp.float32)
    saved_values = []
    for layer_index in range(LAYERS):
        qkv_full, out_turned, up_full, down_turned = weights[layer_index]
        local_qv = lax.dynamic_slice_in_dim(
            qv_bias[layer_index], tp_index * local_width, local_width, 1
        )
        local_up = lax.dynamic_slice_in_dim(
            up_bias[layer_index], tp_index * inner_width, inner_width, 0
        )
        layer_input = stream
        own_hidden = norm_rows(
            stream, norm_gain[layer_index, 0], norm_shift[layer_index, 0]
        ).astype(jnp.bfloat16)
        hidden = halves(own_hidden, swap(own_hidden), first)
        projected = plain(hidden, qkv_full)[:all_rows]
        queries = (projected[:, :local_width] + local_qv[0]).astype(jnp.bfloat16)
        key_rows = projected[:, local_width : 2 * local_width].astype(jnp.bfloat16)
        values = (projected[:, 2 * local_width :] + local_qv[1]).astype(jnp.bfloat16)
        mixed, log_total = attend(queries, key_rows, values, images, local_heads, head_dim)
        mixed = padded(mixed)
        stream = (
            stream
            + shared_sum(back_product, own_rows(mixed), other_rows(mixed), out_turned)
            + out_bias[layer_index, 0]
        )
        middle = stream
        hidden_own = norm_rows(
            stream, norm_gain[layer_index, 1], norm_shift[layer_index, 1]
        ).astype(jnp.bfloat16)
        hidden_other = swap(hidden_own)
        pre_own = plain(hidden_own, up_full) + local_up
        pre_other = plain(hidden_other, up_full) + local_up
        act_other = jax.nn.gelu(pre_other, approximate=False).astype(jnp.bfloat16)
        act_own = jax.nn.gelu(pre_own, approximate=False).astype(jnp.bfloat16)
        stream = (
            stream
            + shared_sum(back_product, act_own, act_other, down_turned)
            + out_bias[layer_index, 1]
        )
        saved_values.append(
            (
                layer_input,
                middle,
                hidden,
                queries,
                key_rows,
                values,
                mixed,
                log_total,
                jnp.concatenate([hidden_own, hidden_other], axis=0),
                pre_own,
                pre_other,
                jnp.concatenate([act_own, act_other], axis=0),
            )
        )
    activations = jnp.where(live, stream, 0.0).astype(jnp.bfloat16)
    grad = jnp.where(live, cotangent.astype(jnp.float32), 0.0)
    owned = []
    gain_grads = [None] * LAYERS
    shift_grads = [None] * LAYERS
    qv_grads = [None] * LAYERS
    out_bias_grads = [None] * LAYERS
    up_bias_grads = [None] * LAYERS
    for layer_index in reversed(range(LAYERS)):
        (
            layer_input,
            middle,
            hidden,
            queries,
            key_rows,
            values,
            mixed,
            log_total,
            hidden_two,
            pre_own,
            pre_other,
            activated,
        ) = saved_values[layer_index]
        qkv_full, out_turned, up_full, down_turned = weights[layer_index]
        branch_own = grad.astype(jnp.bfloat16)
        down_bias_grad = jnp.sum(branch_own.astype(jnp.float32), axis=0)
        branch_other = swap(branch_own)

        def through_gelu(branch, pre):
            act_grad = plain(branch, down_turned)
            gelu_back = jax.vjp(partial(jax.nn.gelu, approximate=False), pre)[1]
            return gelu_back(act_grad)[0].astype(jnp.bfloat16)

        du_own = through_gelu(branch_own, pre_own)
        du_other = through_gelu(branch_other, pre_other)
        norm_grad = shared_sum(back_product, du_own, du_other, up_full)
        pre_grad = jnp.concatenate([du_own, du_other], axis=0)
        branch_both = jnp.concatenate([branch_own, branch_other], axis=0)
        down_grad = row_product(branch_both, activated)
        up_vector_grad = jnp.sum(pre_grad.astype(jnp.float32), axis=0)
        up_grad = row_product(hidden_two, pre_grad)
        norm_back = jax.vjp(
            norm_rows, middle, norm_gain[layer_index, 1], norm_shift[layer_index, 1]
        )[1]
        middle_grad, gain_two, shift_two = norm_back(norm_grad)
        grad = grad + middle_grad
        branch_own = grad.astype(jnp.bfloat16)
        attn_bias_grad = jnp.sum(branch_own.astype(jnp.float32), axis=0)
        branch_full = halves(branch_own, swap(branch_own), first)
        out_grad = row_product(branch_full, mixed)
        mixed_grad = plain(branch_full, out_turned).astype(jnp.bfloat16)[:all_rows]
        stacked = attend_back(
            mixed_grad, queries, key_rows, values, log_total, images, local_heads, head_dim
        )
        stacked = padded(stacked.reshape(all_rows, 3 * local_width))
        stacked_sums = jnp.sum(stacked.astype(jnp.float32), axis=0).reshape(3, local_width)
        norm_grad = shared_sum(back_product, own_rows(stacked), other_rows(stacked), qkv_full)
        qkv_grad = row_product(hidden, stacked)
        norm_back = jax.vjp(
            norm_rows, layer_input, norm_gain[layer_index, 0], norm_shift[layer_index, 0]
        )[1]
        input_part, gain_one, shift_one = norm_back(norm_grad)
        grad = grad + input_part
        if layer_index:
            owned.append(
                (scattered([up_grad, down_grad]), scattered([qkv_grad, out_grad]))
            )
        else:
            joined = scattered([up_grad, down_grad, qkv_grad, out_grad])
            owned.append((joined[:, : 2 * inner_width], joined[:, 2 * inner_width :]))
        gain_grads[layer_index] = jnp.stack([gain_one, gain_two])
        shift_grads[layer_index] = jnp.stack([shift_one, shift_two])
        qv_local = jnp.stack([stacked_sums[0], stacked_sums[2]])
        qv_grads[layer_index] = lax.dynamic_update_slice_in_dim(
            jnp.zeros((2, D), jnp.float32), qv_local, tp_index * local_width, 1
        )
        out_bias_grads[layer_index] = jnp.stack([attn_bias_grad, down_bias_grad])
        up_bias_grads[layer_index] = lax.dynamic_update_slice_in_dim(
            jnp.zeros((FF,), jnp.float32), up_vector_grad, tp_index * inner_width, 0
        ).reshape(FF // D, D)
    small = jnp.concatenate(
        gain_grads + shift_grads + qv_grads + out_bias_grads + up_bias_grads, axis=0
    )
    small = summed_everywhere(small, fsdp_count)
    pair = 2 * LAYERS
    small_totals = [small[pair * k : pair * (k + 1)].reshape(LAYERS, 2, D) for k in range(4)]
    up_totals = small[4 * pair :].reshape(LAYERS, FF)
    owned = owned[::-1]
    up_all = jnp.stack([mlp[:, :inner_width] for mlp, attn in owned])
    down_all = jnp.stack([mlp[:, inner_width:].T for mlp, attn in owned])
    qkv_all = jnp.stack(
        [attn[:, :cut_qkv].reshape(piece_rows, 3, local_width) for mlp, attn in owned]
    )
    out_all = jnp.stack([attn[:, cut_qkv:].T for mlp, attn in owned])
    input_grad = jnp.where(live, grad, 0.0)
    return (
        activations,
        input_grad,
        qkv_all,
        out_all,
        up_all,
        down_all,
        small_totals[0],
        small_totals[1],
        small_totals[2],
        small_totals[3],
        up_totals,
    )


def solution(mesh):
    return jax.shard_map(
        on_device,
        mesh=mesh,
        in_specs=(
            P(("fsdp", "tp"), None),
            P(None, "fsdp", None, "tp"),
            P(None, "tp", "fsdp"),
            P(None, "fsdp", "tp"),
            P(None, "tp", "fsdp"),
            P(),
            P(),
            P(),
            P(),
            P(),
            P(("fsdp", "tp"), None),
        ),
        out_specs=(
            P(("fsdp", "tp"), None),
            P(("fsdp", "tp"), None),
            P(None, "fsdp", None, "tp"),
            P(None, "tp", "fsdp"),
            P(None, "fsdp", "tp"),
            P(None, "tp", "fsdp"),
            P(),
            P(),
            P(),
            P(),
            P(),
        ),
        check_vma=False,
    )
```

```python
import math

import jax
import jax.numpy as jnp
from jax import lax
from jax.experimental import pallas as pl
from jax.experimental.pallas import tpu as pltpu
from jax.sharding import PartitionSpec as P

D = 768
HEADS = 12
FF = 3072
SEQ = 197
LAYERS = 2
IMG_DEV = 3


def norm_rows(value, gain_vector, shift_vector):
    row_mean = jnp.mean(value, axis=-1, keepdims=True)
    centred = value - row_mean
    row_var = jnp.mean(centred * centred, axis=-1, keepdims=True)
    return centred * lax.rsqrt(row_var + 1e-06) * gain_vector + shift_vector


def row_product(left, right):
    return lax.dot_general(
        left, right, (((0,), (0,)), ((), ())), preferred_element_type=jnp.float32
    )


def halves(own, other, first):
    return jnp.concatenate(
        [jnp.where(first, own, other), jnp.where(first, other, own)], axis=0
    )


def swap(value):
    return lax.ppermute(value, "tp", [(0, 1), (1, 0)])


def summed_everywhere(value, fsdp_count):
    step = 1
    while step < fsdp_count:
        value = value + lax.ppermute(
            value, "fsdp", [(place, place ^ step) for place in range(fsdp_count)]
        )
        step *= 2
    return value + swap(value)


def gathered(pieces):
    return lax.all_gather(jnp.concatenate(pieces, axis=1), "fsdp", axis=0, tiled=True)


def scattered(joined):
    return lax.psum_scatter(joined, "fsdp", scatter_dimension=0, tiled=True).astype(jnp.float32)


WINDOW = 208
WINDOW_STEP = 192
LANES = 128
FAR_BELOW = -1e30


def turned_product(left, right):
    return lax.dot_general(
        left, right, (((1,), (1,)), ((), ())), preferred_element_type=jnp.float32
    )


def plain_product(left, right):
    return jnp.dot(left, right, preferred_element_type=jnp.float32)


def window_masks(image):
    low = (SEQ - WINDOW_STEP) * image
    high = low + SEQ
    rows = lax.broadcasted_iota(jnp.int32, (WINDOW, 1), 0)
    columns = lax.broadcasted_iota(jnp.int32, (1, WINDOW), 1)
    return (rows >= low) & (rows < high), (columns >= low) & (columns < high)


def window_chances(query_head, key_pair, row_live, column_live, scale):
    scores = jnp.where(column_live, turned_product(query_head, key_pair) * scale, FAR_BELOW)
    expanded = jnp.exp(scores - jnp.max(scores, axis=-1, keepdims=True))
    total = jnp.sum(expanded, axis=-1, keepdims=True)
    return jnp.where(row_live, expanded / total, 0.0)


def attend_kernel(
    place_ref,
    hidden_ref,
    weight_ref,
    turned_ref,
    bias_ref,
    qkv_ref,
    mixed_ref,
    sent_ref,
    kept_ref,
    mixed_wide,
):
    width = mixed_ref.shape[1]
    row_count = sent_ref.shape[0]
    scale = (D // HEADS) ** (-0.5)
    hidden = hidden_ref[...]
    for part in range(3):
        span = pl.ds(part * width, width)
        product = plain_product(hidden, weight_ref[:, span])
        if part != 1:
            product = product + bias_ref[pl.ds(part // 2, 1), :]
        qkv_ref[:, span] = product.astype(jnp.bfloat16)
    mixed_wide[...] = jnp.zeros_like(mixed_wide)
    lane_low = lax.broadcasted_iota(jnp.int32, (1, LANES), 1) < D // HEADS

    def one_image(image, carry):
        window = pl.ds(pl.multiple_of(image * WINDOW_STEP, 16), WINDOW)
        row_live, column_live = window_masks(image)
        for pair in range(width // LANES):
            query_pair = qkv_ref[window, pl.ds(pair * LANES, LANES)]
            key_pair = qkv_ref[window, pl.ds(width + pair * LANES, LANES)]
            value_pair = qkv_ref[window, pl.ds(2 * width + pair * LANES, LANES)]
            sides = []
            for lane_mask in (lane_low, ~lane_low):
                chances = window_chances(
                    jnp.where(lane_mask, query_pair, jnp.zeros_like(query_pair)),
                    key_pair,
                    row_live,
                    column_live,
                    scale,
                )
                sides.append(plain_product(chances.astype(jnp.bfloat16), value_pair))
            mixed_wide[window, pl.ds(pair * LANES, LANES)] += jnp.where(
                lane_low, sides[0], sides[1]
            )
        return carry

    lax.fori_loop(0, IMG_DEV, one_image, 0)
    mixed_ref[...] = mixed_wide[...].astype(jnp.bfloat16)
    turned = turned_ref[...]
    place = place_ref[0]
    other = pl.ds(pl.multiple_of((1 - place) * row_count, 8), row_count)
    own = pl.ds(pl.multiple_of(place * row_count, 8), row_count)
    sent_ref[...] = turned_product(mixed_wide[other, :].astype(jnp.bfloat16), turned).astype(
        jnp.bfloat16
    )
    kept_ref[...] = turned_product(mixed_wide[own, :].astype(jnp.bfloat16), turned)


def attend_back_kernel(
    place_ref,
    branch_ref,
    qkv_ref,
    weight_ref,
    turned_ref,
    stacked_ref,
    sent_ref,
    kept_ref,
    sums_ref,
    mixed_grad,
    wide,
):
    width = mixed_grad.shape[1]
    row_count = sent_ref.shape[0]
    scale = (D // HEADS) ** (-0.5)
    mixed_grad[...] = plain_product(branch_ref[...], turned_ref[...]).astype(jnp.bfloat16)
    wide[...] = jnp.zeros_like(wide)
    lane_low = lax.broadcasted_iota(jnp.int32, (1, LANES), 1) < D // HEADS

    def one_image(image, carry):
        window = pl.ds(pl.multiple_of(image * WINDOW_STEP, 16), WINDOW)
        row_live, column_live = window_masks(image)
        for pair in range(width // LANES):
            query_pair = qkv_ref[window, pl.ds(pair * LANES, LANES)]
            key_pair = qkv_ref[window, pl.ds(width + pair * LANES, LANES)]
            value_pair = qkv_ref[window, pl.ds(2 * width + pair * LANES, LANES)]
            grad_pair = mixed_grad[window, pl.ds(pair * LANES, LANES)]
            sides = []
            for lane_mask in (lane_low, ~lane_low):
                chances = window_chances(
                    jnp.where(lane_mask, query_pair, jnp.zeros_like(query_pair)),
                    key_pair,
                    row_live,
                    column_live,
                    scale,
                )
                weight_grad = turned_product(
                    jnp.where(lane_mask, grad_pair, jnp.zeros_like(grad_pair)), value_pair
                )
                row_sum = jnp.sum(weight_grad * chances, axis=-1, keepdims=True)
                score_grad = (chances * (weight_grad - row_sum)).astype(jnp.bfloat16)
                sides.append(
                    (
                        plain_product(score_grad, key_pair) * scale,
                        row_product(score_grad, query_pair) * scale,
                        row_product(chances.astype(jnp.bfloat16), grad_pair),
                    )
                )
            for part in range(3):
                wide[window, pl.ds(part * width + pair * LANES, LANES)] += jnp.where(
                    lane_low, sides[0][part], sides[1][part]
                )
        return carry

    lax.fori_loop(0, IMG_DEV, one_image, 0)
    stacked = wide[...].astype(jnp.bfloat16)
    stacked_ref[...] = stacked
    sums_ref[...] = jnp.sum(stacked.astype(jnp.float32), axis=0, keepdims=True)
    place = place_ref[0]
    other = pl.ds(pl.multiple_of((1 - place) * row_count, 8), row_count)
    own = pl.ds(pl.multiple_of(place * row_count, 8), row_count)
    weight = weight_ref[...]
    sent_ref[...] = turned_product(wide[other, :].astype(jnp.bfloat16), weight).astype(jnp.bfloat16)
    kept_ref[...] = turned_product(wide[own, :].astype(jnp.bfloat16), weight)


def attend_grads_kernel(hidden_ref, stacked_ref, branch_ref, mixed_ref, grad_ref):
    cut = stacked_ref.shape[1]
    grad_ref[:, :cut] = row_product(hidden_ref[...], stacked_ref[...]).astype(jnp.bfloat16)
    grad_ref[:, cut:] = row_product(branch_ref[...], mixed_ref[...]).astype(jnp.bfloat16)


def mlp_kernel(hidden_ref, up_ref, turned_ref, bias_ref, act_ref, slope_ref, partial_ref):
    pre = plain_product(hidden_ref[...], up_ref[...]) + bias_ref[...]
    normal = 0.5 * (1.0 + lax.erf(pre * (0.5**0.5)))
    density = jnp.exp(-0.5 * pre * pre) * (0.5 / math.pi) ** 0.5
    active = (pre * normal).astype(jnp.bfloat16)
    act_ref[...] = active
    slope_ref[...] = (normal + pre * density).astype(jnp.bfloat16)
    partial_ref[...] = turned_product(active, turned_ref[...]).astype(partial_ref.dtype)


def mlp_back_kernel(branch_ref, slope_ref, turned_ref, up_ref, pre_ref, partial_ref, sums_ref):
    act_grad = plain_product(branch_ref[...], turned_ref[...])
    pre_grad = (act_grad * slope_ref[...].astype(jnp.float32)).astype(jnp.bfloat16)
    pre_ref[...] = pre_grad
    partial_ref[...] = turned_product(pre_grad, up_ref[...]).astype(partial_ref.dtype)
    sums_ref[...] = jnp.sum(pre_grad.astype(jnp.float32), axis=0, keepdims=True)


def mlp_grads_kernel(
    hidden_own, hidden_other, pre_own, pre_other, branch_own, branch_other, act_own, act_other, grad_ref
):
    cut = pre_own.shape[1]
    grad_ref[:, :cut] = (
        row_product(hidden_own[...], pre_own[...]) + row_product(hidden_other[...], pre_other[...])
    ).astype(jnp.bfloat16)
    grad_ref[:, cut:] = (
        row_product(branch_own[...], act_own[...]) + row_product(branch_other[...], act_other[...])
    ).astype(jnp.bfloat16)


ROOM = 60 * 1024 * 1024


def columns(array, width, place):
    return array, pl.BlockSpec((array.shape[0], width), lambda step: (0, place))


def whole(array):
    return array, pl.BlockSpec(array.shape, lambda step: (0,) * array.ndim)


def scalar(array):
    return array, pl.BlockSpec(memory_space=pltpu.SMEM)


def run_kernel(kernel, operands, results, scratch=(), name=None, flops=0):
    outs = [jax.ShapeDtypeStruct(shape, dtype) for shape, dtype in results]
    return pl.pallas_call(
        kernel,
        grid=(1,),
        in_specs=[spec for array, spec in operands],
        out_specs=[pl.BlockSpec(shape, lambda step, rank=len(shape): (0,) * rank) for shape, dtype in results],
        out_shape=outs,
        scratch_shapes=list(scratch),
        compiler_params=pltpu.CompilerParams(vmem_limit_bytes=ROOM),
        cost_estimate=pl.CostEstimate(
            flops=flops,
            transcendentals=0,
            bytes_accessed=sum(math.prod(out.shape) * out.dtype.itemsize for out in outs),
        ),
        name=name,
    )(*[array for array, spec in operands])


def on_device(
    tokens,
    qkv_weight,
    out_weight,
    up_weight,
    down_weight,
    norm_gain,
    norm_shift,
    qv_bias,
    out_bias,
    up_bias,
    cotangent,
):
    tp_index = lax.axis_index("tp")
    tp_count = lax.axis_size("tp")
    fsdp_count = lax.axis_size("fsdp")
    row_count = tokens.shape[0]
    local_width = qkv_weight.shape[3]
    inner_width = up_weight.shape[2]
    piece_rows = qkv_weight.shape[1]
    all_rows = IMG_DEV * SEQ
    slot_rows = row_count * tp_count
    first = tp_index == 0
    live = (tp_index * row_count + jnp.arange(row_count) < all_rows)[:, None]
    cut_qkv = 3 * local_width
    cut_out = cut_qkv + local_width

    place = jnp.reshape(tp_index, (1,)).astype(jnp.int32)
    bf16 = jnp.bfloat16
    f32 = jnp.float32

    def attn_pieces(layer_index):
        return [
            qkv_weight[layer_index].reshape(piece_rows, cut_qkv),
            out_weight[layer_index].T,
        ]

    def mlp_pieces(layer_index):
        return [up_weight[layer_index], down_weight[layer_index].T]

    attn_zero = gathered(attn_pieces(0))
    mlp_zero = gathered(mlp_pieces(0))
    full_one = gathered(attn_pieces(1) + mlp_pieces(1))
    sources = [
        (attn_zero, mlp_zero, 0, 1),
        (full_one, full_one, 1, 2),
    ]

    stream = tokens.astype(jnp.float32)
    saved_values = []
    for layer_index in range(LAYERS):
        attn_full, mlp_full, up_place, down_place = sources[layer_index]
        qkv_side = columns(attn_full, cut_qkv, 0)
        out_side = columns(attn_full, local_width, 3)
        up_side = columns(mlp_full, inner_width, up_place)
        down_side = columns(mlp_full, inner_width, down_place)
        local_qv = lax.dynamic_slice_in_dim(
            qv_bias[layer_index], tp_index * local_width, local_width, 1
        )
        local_up = lax.dynamic_slice_in_dim(
            up_bias[layer_index], tp_index * inner_width, inner_width, 0
        )[None]
        layer_input = stream
        own_hidden = norm_rows(
            stream, norm_gain[layer_index, 0], norm_shift[layer_index, 0]
        ).astype(bf16)
        hidden = halves(own_hidden, swap(own_hidden), first)
        qkv, mixed, sent, kept = run_kernel(
            attend_kernel,
            [scalar(place), whole(hidden), qkv_side, out_side, whole(local_qv)],
            [
                ((slot_rows, cut_qkv), bf16),
                ((slot_rows, local_width), bf16),
                ((row_count, D), bf16),
                ((row_count, D), f32),
            ],
            [pltpu.VMEM((slot_rows, local_width), f32)],
            name="attend",
        )
        stream = stream + (kept + swap(sent).astype(f32)) + out_bias[layer_index, 0]
        middle = stream
        hidden_own = norm_rows(
            stream, norm_gain[layer_index, 1], norm_shift[layer_index, 1]
        ).astype(bf16)
        hidden_other = swap(hidden_own)

        def mlp_half(hidden_half, kind):
            return run_kernel(
                mlp_kernel,
                [whole(hidden_half), up_side, down_side, whole(local_up)],
                [
                    ((row_count, inner_width), bf16),
                    ((row_count, inner_width), bf16),
                    ((row_count, D), kind),
                ],
                name="mlp",
            )

        act_own, slope_own, kept = mlp_half(hidden_own, f32)
        act_other, slope_other, sent = mlp_half(hidden_other, bf16)
        stream = stream + (kept + swap(sent).astype(f32)) + out_bias[layer_index, 1]
        saved_values.append(
            (
                layer_input,
                middle,
                hidden,
                qkv,
                mixed,
                hidden_own,
                hidden_other,
                slope_own,
                slope_other,
                act_own,
                act_other,
                (qkv_side, out_side, up_side, down_side),
            )
        )
    activations = jnp.where(live, stream, 0.0).astype(jnp.bfloat16)
    grad = jnp.where(live, cotangent.astype(jnp.float32), 0.0)
    owned = []
    gain_grads = [None] * LAYERS
    shift_grads = [None] * LAYERS
    qv_grads = [None] * LAYERS
    out_bias_grads = [None] * LAYERS
    up_bias_grads = [None] * LAYERS
    for layer_index in reversed(range(LAYERS)):
        (
            layer_input,
            middle,
            hidden,
            qkv,
            mixed,
            hidden_own,
            hidden_other,
            slope_own,
            slope_other,
            act_own,
            act_other,
            (qkv_side, out_side, up_side, down_side),
        ) = saved_values[layer_index]
        branch_own = grad.astype(bf16)
        down_bias_grad = jnp.sum(branch_own.astype(f32), axis=0)
        branch_other = swap(branch_own)

        def mlp_half_back(branch, slope, kind):
            return run_kernel(
                mlp_back_kernel,
                [whole(branch), whole(slope), down_side, up_side],
                [((row_count, inner_width), bf16), ((row_count, D), kind), ((1, inner_width), f32)],
                name="mlp_back",
            )

        pre_own, kept, up_sums_own = mlp_half_back(branch_own, slope_own, f32)
        pre_other, sent, up_sums_other = mlp_half_back(branch_other, slope_other, bf16)
        norm_grad = kept + swap(sent).astype(f32)
        up_vector_grad = (up_sums_own + up_sums_other)[0]
        (mlp_grad,) = run_kernel(
            mlp_grads_kernel,
            [
                whole(part)
                for part in (
                    hidden_own,
                    hidden_other,
                    pre_own,
                    pre_other,
                    branch_own,
                    branch_other,
                    act_own,
                    act_other,
                )
            ],
            [((D, 2 * inner_width), bf16)],
            name="mlp_grads",
        )
        norm_back = jax.vjp(
            norm_rows, middle, norm_gain[layer_index, 1], norm_shift[layer_index, 1]
        )[1]
        middle_grad, gain_two, shift_two = norm_back(norm_grad)
        grad = grad + middle_grad
        branch_own = grad.astype(bf16)
        attn_bias_grad = jnp.sum(branch_own.astype(f32), axis=0)
        branch_full = halves(branch_own, swap(branch_own), first)
        stacked, sent, kept, stacked_sums = run_kernel(
            attend_back_kernel,
            [scalar(place), whole(branch_full), whole(qkv), qkv_side, out_side],
            [
                ((slot_rows, cut_qkv), bf16),
                ((row_count, D), bf16),
                ((row_count, D), f32),
                ((1, cut_qkv), f32),
            ],
            [pltpu.VMEM((slot_rows, local_width), bf16), pltpu.VMEM((slot_rows, cut_qkv), f32)],
            name="attend_back",
        )
        norm_grad = kept + swap(sent).astype(f32)
        stacked_sums = stacked_sums.reshape(3, local_width)
        (attn_grad,) = run_kernel(
            attend_grads_kernel,
            [whole(hidden), whole(stacked), whole(branch_full), whole(mixed)],
            [((D, cut_out), bf16)],
            name="attend_grads",
        )
        norm_back = jax.vjp(
            norm_rows, layer_input, norm_gain[layer_index, 0], norm_shift[layer_index, 0]
        )[1]
        input_part, gain_one, shift_one = norm_back(norm_grad)
        grad = grad + input_part
        if layer_index:
            owned.append((scattered(mlp_grad), scattered(attn_grad)))
        else:
            joined = scattered(jnp.concatenate([mlp_grad, attn_grad], axis=1))
            owned.append((joined[:, : 2 * inner_width], joined[:, 2 * inner_width :]))
        gain_grads[layer_index] = jnp.stack([gain_one, gain_two])
        shift_grads[layer_index] = jnp.stack([shift_one, shift_two])
        qv_local = jnp.stack([stacked_sums[0], stacked_sums[2]])
        qv_grads[layer_index] = lax.dynamic_update_slice_in_dim(
            jnp.zeros((2, D), jnp.float32), qv_local, tp_index * local_width, 1
        )
        out_bias_grads[layer_index] = jnp.stack([attn_bias_grad, down_bias_grad])
        up_bias_grads[layer_index] = lax.dynamic_update_slice_in_dim(
            jnp.zeros((FF,), jnp.float32), up_vector_grad, tp_index * inner_width, 0
        ).reshape(FF // D, D)
    small = jnp.concatenate(
        gain_grads + shift_grads + qv_grads + out_bias_grads + up_bias_grads, axis=0
    )
    small = summed_everywhere(small, fsdp_count)
    pair = 2 * LAYERS
    small_totals = [small[pair * k : pair * (k + 1)].reshape(LAYERS, 2, D) for k in range(4)]
    up_totals = small[4 * pair :].reshape(LAYERS, FF)
    owned = owned[::-1]
    up_all = jnp.stack([mlp[:, :inner_width] for mlp, attn in owned])
    down_all = jnp.stack([mlp[:, inner_width:].T for mlp, attn in owned])
    qkv_all = jnp.stack(
        [attn[:, :cut_qkv].reshape(piece_rows, 3, local_width) for mlp, attn in owned]
    )
    out_all = jnp.stack([attn[:, cut_qkv:].T for mlp, attn in owned])
    input_grad = jnp.where(live, grad, 0.0)
    return (
        activations,
        input_grad,
        qkv_all,
        out_all,
        up_all,
        down_all,
        small_totals[0],
        small_totals[1],
        small_totals[2],
        small_totals[3],
        up_totals,
    )


def solution(mesh):
    return jax.shard_map(
        on_device,
        mesh=mesh,
        in_specs=(
            P(("fsdp", "tp"), None),
            P(None, "fsdp", None, "tp"),
            P(None, "tp", "fsdp"),
            P(None, "fsdp", "tp"),
            P(None, "tp", "fsdp"),
            P(),
            P(),
            P(),
            P(),
            P(),
            P(("fsdp", "tp"), None),
        ),
        out_specs=(
            P(("fsdp", "tp"), None),
            P(("fsdp", "tp"), None),
            P(None, "fsdp", None, "tp"),
            P(None, "tp", "fsdp"),
            P(None, "fsdp", "tp"),
            P(None, "tp", "fsdp"),
            P(),
            P(),
            P(),
            P(),
            P(),
        ),
        check_vma=False,
    )
```

```python
import math

import jax
import jax.numpy as jnp
from jax import lax
from jax.experimental import pallas as pl
from jax.experimental.pallas import tpu as pltpu
from jax.sharding import PartitionSpec as P

D = 768
HEADS = 12
FF = 3072
SEQ = 197
LAYERS = 2
IMG_DEV = 3


def norm_rows(value, gain_vector, shift_vector):
    row_mean = jnp.mean(value, axis=-1, keepdims=True)
    centred = value - row_mean
    row_var = jnp.mean(centred * centred, axis=-1, keepdims=True)
    return centred * lax.rsqrt(row_var + 1e-06) * gain_vector + shift_vector


def row_product(left, right):
    return lax.dot_general(
        left, right, (((0,), (0,)), ((), ())), preferred_element_type=jnp.float32
    )


def swap(value):
    return lax.ppermute(value, "tp", [(0, 1), (1, 0)])


def summed_everywhere(value, fsdp_count):
    step = 1
    while step < fsdp_count:
        value = value + lax.ppermute(
            value, "fsdp", [(place, place ^ step) for place in range(fsdp_count)]
        )
        step *= 2
    return value + swap(value)


def halved(value, fsdp_count):
    index = lax.axis_index("fsdp")
    step = 1
    while step < fsdp_count:
        side = (index // step) % 2
        value = value.reshape(fsdp_count // (2 * step), 2, -1, value.shape[-1])
        sent = lax.ppermute(
            lax.dynamic_index_in_dim(value, 1 - side, 1, keepdims=False),
            "fsdp",
            [(place, place ^ step) for place in range(fsdp_count)],
        )
        kept = lax.dynamic_index_in_dim(value, side, 1, keepdims=False)
        value = kept.astype(jnp.float32) + sent.astype(jnp.float32)
        step *= 2
        if step < fsdp_count:
            value = value.astype(jnp.bfloat16)
    return value.reshape(-1, value.shape[-1])


def gathered(pieces):
    return lax.all_gather(jnp.concatenate(pieces, axis=1), "fsdp", axis=0, tiled=True)


def scattered(joined):
    return lax.psum_scatter(joined, "fsdp", scatter_dimension=0, tiled=True).astype(jnp.float32)


WINDOW = 208
WINDOW_STEP = 192
LANES = 128
FAR_BELOW = -1e30


def turned_product(left, right):
    return lax.dot_general(
        left, right, (((1,), (1,)), ((), ())), preferred_element_type=jnp.float32
    )


def plain_product(left, right):
    return jnp.dot(left, right, preferred_element_type=jnp.float32)


def window_masks(image):
    low = (SEQ - WINDOW_STEP) * image
    high = low + SEQ
    rows = lax.broadcasted_iota(jnp.int32, (WINDOW, 1), 0)
    columns = lax.broadcasted_iota(jnp.int32, (1, WINDOW), 1)
    return (rows >= low) & (rows < high), (columns >= low) & (columns < high)


def window_chances(query_head, key_pair, row_live, column_live, scale):
    scores = jnp.where(column_live, turned_product(query_head, key_pair) * scale, FAR_BELOW)
    expanded = jnp.exp(scores - jnp.max(scores, axis=-1, keepdims=True))
    total = jnp.sum(expanded, axis=-1, keepdims=True)
    return jnp.where(row_live, expanded / total, 0.0)


def attend_kernel(
    place_ref,
    hidden_own_ref,
    hidden_other_ref,
    weights_ref,
    bias_ref,
    qkv_ref,
    mixed_own_ref,
    mixed_other_ref,
    sent_ref,
    kept_ref,
    mixed_wide,
    wide,
):
    width = mixed_own_ref.shape[1]
    row_count = sent_ref.shape[0]
    scale = (D // HEADS) ** (-0.5)
    place = place_ref[0]
    other = pl.ds(pl.multiple_of((1 - place) * row_count, 8), row_count)
    own = pl.ds(pl.multiple_of(place * row_count, 8), row_count)
    for part in range(3):
        span = pl.ds(part * width, width)
        for rows, hidden_ref in ((own, hidden_own_ref), (other, hidden_other_ref)):
            product = plain_product(hidden_ref[...], weights_ref[:, span])
            if part != 1:
                product = product + bias_ref[pl.ds(part // 2, 1), :]
            wide[rows, span] = product
    qkv_ref[...] = wide[...].astype(jnp.bfloat16)
    mixed_wide[...] = jnp.zeros_like(mixed_wide)
    lane_low = lax.broadcasted_iota(jnp.int32, (1, LANES), 1) < D // HEADS

    def one_image(image, carry):
        window = pl.ds(pl.multiple_of(image * WINDOW_STEP, 16), WINDOW)
        row_live, column_live = window_masks(image)
        for pair in range(width // LANES):
            query_pair = qkv_ref[window, pl.ds(pair * LANES, LANES)]
            key_pair = qkv_ref[window, pl.ds(width + pair * LANES, LANES)]
            value_pair = qkv_ref[window, pl.ds(2 * width + pair * LANES, LANES)]
            sides = []
            for lane_mask in (lane_low, ~lane_low):
                chances = window_chances(
                    jnp.where(lane_mask, query_pair, jnp.zeros_like(query_pair)),
                    key_pair,
                    row_live,
                    column_live,
                    scale,
                )
                sides.append(plain_product(chances.astype(jnp.bfloat16), value_pair))
            mixed_wide[window, pl.ds(pair * LANES, LANES)] += jnp.where(
                lane_low, sides[0], sides[1]
            )
        return carry

    lax.fori_loop(0, IMG_DEV, one_image, 0)
    turned = weights_ref[:, 3 * width :]
    mixed_own = mixed_wide[own, :].astype(jnp.bfloat16)
    mixed_other = mixed_wide[other, :].astype(jnp.bfloat16)
    mixed_own_ref[...] = mixed_own
    mixed_other_ref[...] = mixed_other
    sent_ref[...] = turned_product(mixed_other, turned).astype(jnp.bfloat16)
    kept_ref[...] = turned_product(mixed_own, turned)


def attend_back_kernel(
    place_ref,
    branch_own_ref,
    branch_other_ref,
    qkv_ref,
    weights_ref,
    stacked_own_ref,
    stacked_other_ref,
    sent_ref,
    kept_ref,
    sums_ref,
    mixed_grad,
    wide,
):
    width = mixed_grad.shape[1]
    row_count = sent_ref.shape[0]
    scale = (D // HEADS) ** (-0.5)
    place = place_ref[0]
    other = pl.ds(pl.multiple_of((1 - place) * row_count, 8), row_count)
    own = pl.ds(pl.multiple_of(place * row_count, 8), row_count)
    turned = weights_ref[:, 3 * width :]
    wide[own, :width] = plain_product(branch_own_ref[...], turned)
    wide[other, :width] = plain_product(branch_other_ref[...], turned)
    mixed_grad[...] = wide[:, :width].astype(jnp.bfloat16)
    wide[...] = jnp.zeros_like(wide)
    lane_low = lax.broadcasted_iota(jnp.int32, (1, LANES), 1) < D // HEADS

    def one_image(image, carry):
        window = pl.ds(pl.multiple_of(image * WINDOW_STEP, 16), WINDOW)
        row_live, column_live = window_masks(image)
        for pair in range(width // LANES):
            query_pair = qkv_ref[window, pl.ds(pair * LANES, LANES)]
            key_pair = qkv_ref[window, pl.ds(width + pair * LANES, LANES)]
            value_pair = qkv_ref[window, pl.ds(2 * width + pair * LANES, LANES)]
            grad_pair = mixed_grad[window, pl.ds(pair * LANES, LANES)]
            sides = []
            for lane_mask in (lane_low, ~lane_low):
                chances = window_chances(
                    jnp.where(lane_mask, query_pair, jnp.zeros_like(query_pair)),
                    key_pair,
                    row_live,
                    column_live,
                    scale,
                )
                weight_grad = turned_product(
                    jnp.where(lane_mask, grad_pair, jnp.zeros_like(grad_pair)), value_pair
                )
                row_sum = jnp.sum(weight_grad * chances, axis=-1, keepdims=True)
                score_grad = (chances * (weight_grad - row_sum)).astype(jnp.bfloat16)
                sides.append(
                    (
                        plain_product(score_grad, key_pair) * scale,
                        row_product(score_grad, query_pair) * scale,
                        row_product(chances.astype(jnp.bfloat16), grad_pair),
                    )
                )
            for part in range(3):
                wide[window, pl.ds(part * width + pair * LANES, LANES)] += jnp.where(
                    lane_low, sides[0][part], sides[1][part]
                )
        return carry

    lax.fori_loop(0, IMG_DEV, one_image, 0)
    weight = weights_ref[:, : 3 * width]
    stacked_own = wide[own, :].astype(jnp.bfloat16)
    stacked_other = wide[other, :].astype(jnp.bfloat16)
    stacked_own_ref[...] = stacked_own
    stacked_other_ref[...] = stacked_other
    sums_ref[...] = jnp.sum(stacked_own.astype(jnp.float32), axis=0, keepdims=True) + jnp.sum(
        stacked_other.astype(jnp.float32), axis=0, keepdims=True
    )
    sent_ref[...] = turned_product(stacked_other, weight).astype(jnp.bfloat16)
    kept_ref[...] = turned_product(stacked_own, weight)


def mlp_kernel(hidden_ref, up_ref, turned_ref, bias_ref, act_ref, slope_ref, partial_ref):
    pre = plain_product(hidden_ref[...], up_ref[...]) + bias_ref[...]
    normal = 0.5 * (1.0 + lax.erf(pre * (0.5**0.5)))
    density = jnp.exp(-0.5 * pre * pre) * (0.5 / math.pi) ** 0.5
    active = (pre * normal).astype(jnp.bfloat16)
    act_ref[...] = active
    slope_ref[...] = (normal + pre * density).astype(jnp.bfloat16)
    partial_ref[...] = turned_product(active, turned_ref[...]).astype(partial_ref.dtype)


def mlp_back_kernel(branch_ref, slope_ref, turned_ref, up_ref, pre_ref, partial_ref, sums_ref):
    act_grad = plain_product(branch_ref[...], turned_ref[...])
    pre_grad = (act_grad * slope_ref[...].astype(jnp.float32)).astype(jnp.bfloat16)
    pre_ref[...] = pre_grad
    partial_ref[...] = turned_product(pre_grad, up_ref[...]).astype(partial_ref.dtype)
    sums_ref[...] = jnp.sum(pre_grad.astype(jnp.float32), axis=0, keepdims=True)


def grads_kernel(*refs):
    first_left, first_right, second_left, second_right = (
        (refs[2 * pair], refs[2 * pair + 1]) for pair in range(4)
    )
    grad_ref = refs[-1]
    cut = first_right[0].shape[1]
    for span, lefts, rights in (
        (slice(0, cut), first_left, first_right),
        (slice(cut, None), second_left, second_right),
    ):
        grad_ref[:, span] = sum(
            row_product(left[...], right[...]) for left, right in zip(lefts, rights)
        ).astype(jnp.bfloat16)


ROOM = 60 * 1024 * 1024


def columns(array, width, place):
    return array, pl.BlockSpec((array.shape[0], width), lambda step: (0, place))


def whole(array):
    return array, pl.BlockSpec(array.shape, lambda step: (0,) * array.ndim)


def scalar(array):
    return array, pl.BlockSpec(memory_space=pltpu.SMEM)


def run_kernel(kernel, operands, results, scratch=(), name=None, flops=0):
    outs = [jax.ShapeDtypeStruct(shape, dtype) for shape, dtype in results]
    return pl.pallas_call(
        kernel,
        grid=(1,),
        in_specs=[spec for array, spec in operands],
        out_specs=[pl.BlockSpec(shape, lambda step, rank=len(shape): (0,) * rank) for shape, dtype in results],
        out_shape=outs,
        scratch_shapes=list(scratch),
        compiler_params=pltpu.CompilerParams(vmem_limit_bytes=ROOM),
        cost_estimate=pl.CostEstimate(
            flops=flops,
            transcendentals=0,
            bytes_accessed=sum(math.prod(out.shape) * out.dtype.itemsize for out in outs),
        ),
        name=name,
    )(*[array for array, spec in operands])


def packed_grads(pairs, total, width, place, held=None):
    operands = [whole(part) for pair in pairs for part in pair]
    aliases = {}
    if held is not None:
        aliases = {len(operands): 0}
        operands.append((held, pl.BlockSpec(memory_space=pl.ANY)))
    return pl.pallas_call(
        grads_kernel,
        grid=(1,),
        in_specs=[spec for array, spec in operands],
        out_specs=pl.BlockSpec((D, width), lambda step: (0, place)),
        out_shape=jax.ShapeDtypeStruct((D, total), jnp.bfloat16),
        input_output_aliases=aliases,
        compiler_params=pltpu.CompilerParams(vmem_limit_bytes=ROOM),
        name="packed_grads",
    )(*[array for array, spec in operands])


def on_device(
    tokens,
    qkv_weight,
    out_weight,
    up_weight,
    down_weight,
    norm_gain,
    norm_shift,
    qv_bias,
    out_bias,
    up_bias,
    cotangent,
):
    tp_index = lax.axis_index("tp")
    tp_count = lax.axis_size("tp")
    fsdp_count = lax.axis_size("fsdp")
    row_count = tokens.shape[0]
    local_width = qkv_weight.shape[3]
    inner_width = up_weight.shape[2]
    piece_rows = qkv_weight.shape[1]
    all_rows = IMG_DEV * SEQ
    slot_rows = row_count * tp_count
    live = (tp_index * row_count + jnp.arange(row_count) < all_rows)[:, None]
    cut_qkv = 3 * local_width
    cut_out = cut_qkv + local_width

    place = jnp.reshape(tp_index, (1,)).astype(jnp.int32)
    bf16 = jnp.bfloat16
    f32 = jnp.float32

    def attn_pieces(layer_index):
        return [
            qkv_weight[layer_index].reshape(piece_rows, cut_qkv),
            out_weight[layer_index].T,
        ]

    def mlp_pieces(layer_index):
        return [up_weight[layer_index], down_weight[layer_index].T]

    attn_zero = gathered(attn_pieces(0))
    middle_full = gathered(mlp_pieces(0) + attn_pieces(1))
    mlp_one = gathered(mlp_pieces(1))
    joint = 2 * inner_width + cut_out
    sources = [
        (columns(attn_zero, cut_out, 0), columns(middle_full, inner_width, 0), columns(middle_full, inner_width, 1)),
        (columns(middle_full, cut_out, 2), columns(mlp_one, inner_width, 0), columns(mlp_one, inner_width, 1)),
    ]

    stream = tokens.astype(jnp.float32)
    saved_values = []
    for layer_index in range(LAYERS):
        attn_side, up_side, down_side = sources[layer_index]
        local_qv = lax.dynamic_slice_in_dim(
            qv_bias[layer_index], tp_index * local_width, local_width, 1
        )
        local_up = lax.dynamic_slice_in_dim(
            up_bias[layer_index], tp_index * inner_width, inner_width, 0
        )[None]
        layer_input = stream
        own_hidden = norm_rows(
            stream, norm_gain[layer_index, 0], norm_shift[layer_index, 0]
        ).astype(bf16)
        other_hidden = swap(own_hidden)
        qkv, mixed_own, mixed_other, sent, kept = run_kernel(
            attend_kernel,
            [scalar(place), whole(own_hidden), whole(other_hidden), attn_side, whole(local_qv)],
            [
                ((slot_rows, cut_qkv), bf16),
                ((row_count, local_width), bf16),
                ((row_count, local_width), bf16),
                ((row_count, D), bf16),
                ((row_count, D), f32),
            ],
            [pltpu.VMEM((slot_rows, local_width), f32), pltpu.VMEM((slot_rows, cut_qkv), f32)],
            name="attend",
        )
        stream = stream + (kept + swap(sent).astype(f32)) + out_bias[layer_index, 0]
        middle = stream
        hidden_own = norm_rows(
            stream, norm_gain[layer_index, 1], norm_shift[layer_index, 1]
        ).astype(bf16)
        hidden_other = swap(hidden_own)

        def mlp_half(hidden_half, kind):
            return run_kernel(
                mlp_kernel,
                [whole(hidden_half), up_side, down_side, whole(local_up)],
                [
                    ((row_count, inner_width), bf16),
                    ((row_count, inner_width), bf16),
                    ((row_count, D), kind),
                ],
                name="mlp",
            )

        act_own, slope_own, kept = mlp_half(hidden_own, f32)
        act_other, slope_other, sent = mlp_half(hidden_other, bf16)
        stream = stream + (kept + swap(sent).astype(f32)) + out_bias[layer_index, 1]
        saved_values.append(
            (
                layer_input,
                middle,
                (own_hidden, other_hidden),
                qkv,
                (mixed_own, mixed_other),
                hidden_own,
                hidden_other,
                slope_own,
                slope_other,
                act_own,
                act_other,
                (attn_side, up_side, down_side),
            )
        )
    activations = jnp.where(live, stream, 0.0).astype(jnp.bfloat16)
    grad = jnp.where(live, cotangent.astype(jnp.float32), 0.0)
    held = None
    scattered_grads = []
    gain_grads = [None] * LAYERS
    shift_grads = [None] * LAYERS
    qv_grads = [None] * LAYERS
    out_bias_grads = [None] * LAYERS
    up_bias_grads = [None] * LAYERS
    for layer_index in reversed(range(LAYERS)):
        (
            layer_input,
            middle,
            hidden_pair,
            qkv,
            mixed_pair,
            hidden_own,
            hidden_other,
            slope_own,
            slope_other,
            act_own,
            act_other,
            (attn_side, up_side, down_side),
        ) = saved_values[layer_index]
        branch_own = grad.astype(bf16)
        down_bias_grad = jnp.sum(branch_own.astype(f32), axis=0)
        branch_other = swap(branch_own)

        def mlp_half_back(branch, slope, kind):
            return run_kernel(
                mlp_back_kernel,
                [whole(branch), whole(slope), down_side, up_side],
                [((row_count, inner_width), bf16), ((row_count, D), kind), ((1, inner_width), f32)],
                name="mlp_back",
            )

        pre_own, kept, up_sums_own = mlp_half_back(branch_own, slope_own, f32)
        pre_other, sent, up_sums_other = mlp_half_back(branch_other, slope_other, bf16)
        up_vector_grad = (up_sums_own + up_sums_other)[0]
        mlp_grad = packed_grads(
            [
                (hidden_own, hidden_other),
                (pre_own, pre_other),
                (branch_own, branch_other),
                (act_own, act_other),
            ],
            2 * inner_width if held is None else joint,
            2 * inner_width,
            0,
            held,
        )
        received, mlp_grad = lax.optimization_barrier((swap(sent), mlp_grad))
        norm_grad = kept + received.astype(f32)
        scattered_grads.append(scattered(mlp_grad))
        norm_back = jax.vjp(
            norm_rows, middle, norm_gain[layer_index, 1], norm_shift[layer_index, 1]
        )[1]
        middle_grad, gain_two, shift_two = norm_back(norm_grad)
        grad = grad + middle_grad
        branch_own = grad.astype(bf16)
        attn_bias_grad = jnp.sum(branch_own.astype(f32), axis=0)
        branch_other = swap(branch_own)
        stacked_own, stacked_other, sent, kept, stacked_sums = run_kernel(
            attend_back_kernel,
            [scalar(place), whole(branch_own), whole(branch_other), whole(qkv), attn_side],
            [
                ((row_count, cut_qkv), bf16),
                ((row_count, cut_qkv), bf16),
                ((row_count, D), bf16),
                ((row_count, D), f32),
                ((1, cut_qkv), f32),
            ],
            [pltpu.VMEM((slot_rows, local_width), bf16), pltpu.VMEM((slot_rows, cut_qkv), f32)],
            name="attend_back",
        )
        stacked_sums = stacked_sums.reshape(3, local_width)
        attn_grad = packed_grads(
            [hidden_pair, (stacked_own, stacked_other), (branch_own, branch_other), mixed_pair],
            joint if layer_index else cut_out,
            cut_out,
            2 if layer_index else 0,
        )
        received, attn_grad = lax.optimization_barrier((swap(sent), attn_grad))
        norm_grad = kept + received.astype(f32)
        held = attn_grad
        norm_back = jax.vjp(
            norm_rows, layer_input, norm_gain[layer_index, 0], norm_shift[layer_index, 0]
        )[1]
        input_part, gain_one, shift_one = norm_back(norm_grad)
        grad = grad + input_part
        gain_grads[layer_index] = jnp.stack([gain_one, gain_two])
        shift_grads[layer_index] = jnp.stack([shift_one, shift_two])
        qv_local = jnp.stack([stacked_sums[0], stacked_sums[2]])
        qv_grads[layer_index] = lax.dynamic_update_slice_in_dim(
            jnp.zeros((2, D), jnp.float32), qv_local, tp_index * local_width, 1
        )
        out_bias_grads[layer_index] = jnp.stack([attn_bias_grad, down_bias_grad])
        up_bias_grads[layer_index] = lax.dynamic_update_slice_in_dim(
            jnp.zeros((FF,), jnp.float32), up_vector_grad, tp_index * inner_width, 0
        ).reshape(FF // D, D)
    small = jnp.concatenate(
        gain_grads + shift_grads + qv_grads + out_bias_grads + up_bias_grads, axis=0
    )
    small = summed_everywhere(small, fsdp_count)
    pair = 2 * LAYERS
    small_totals = [small[pair * k : pair * (k + 1)].reshape(LAYERS, 2, D) for k in range(4)]
    up_totals = small[4 * pair :].reshape(LAYERS, FF)
    mlp_last, joint_owned = scattered_grads
    attn_first = halved(held, fsdp_count)
    owned = [
        (joint_owned[:, : 2 * inner_width], attn_first),
        (mlp_last, joint_owned[:, 2 * inner_width :]),
    ]
    up_all = jnp.stack([mlp[:, :inner_width] for mlp, attn in owned])
    down_all = jnp.stack([mlp[:, inner_width:].T for mlp, attn in owned])
    qkv_all = jnp.stack(
        [attn[:, :cut_qkv].reshape(piece_rows, 3, local_width) for mlp, attn in owned]
    )
    out_all = jnp.stack([attn[:, cut_qkv:].T for mlp, attn in owned])
    input_grad = jnp.where(live, grad, 0.0)
    return (
        activations,
        input_grad,
        qkv_all,
        out_all,
        up_all,
        down_all,
        small_totals[0],
        small_totals[1],
        small_totals[2],
        small_totals[3],
        up_totals,
    )


def solution(mesh):
    return jax.shard_map(
        on_device,
        mesh=mesh,
        in_specs=(
            P(("fsdp", "tp"), None),
            P(None, "fsdp", None, "tp"),
            P(None, "tp", "fsdp"),
            P(None, "fsdp", "tp"),
            P(None, "tp", "fsdp"),
            P(),
            P(),
            P(),
            P(),
            P(),
            P(("fsdp", "tp"), None),
        ),
        out_specs=(
            P(("fsdp", "tp"), None),
            P(("fsdp", "tp"), None),
            P(None, "fsdp", None, "tp"),
            P(None, "tp", "fsdp"),
            P(None, "fsdp", "tp"),
            P(None, "tp", "fsdp"),
            P(),
            P(),
            P(),
            P(),
            P(),
        ),
        check_vma=False,
    )
```

```python
import math

import jax
import jax.numpy as jnp
from jax import lax
from jax.experimental import pallas as pl
from jax.experimental.pallas import tpu as pltpu
from jax.sharding import PartitionSpec as P

D = 768
HEADS = 12
FF = 3072
SEQ = 197
LAYERS = 2
IMG_DEV = 3


def norm_rows(value, gain_vector, shift_vector):
    row_mean = jnp.mean(value, axis=-1, keepdims=True)
    centred = value - row_mean
    row_var = jnp.mean(centred * centred, axis=-1, keepdims=True)
    return centred * lax.rsqrt(row_var + 1e-06) * gain_vector + shift_vector


def row_product(left, right):
    return lax.dot_general(
        left, right, (((0,), (0,)), ((), ())), preferred_element_type=jnp.float32
    )


def swap(value):
    return lax.ppermute(value, "tp", [(0, 1), (1, 0)])


def reduced_together(value, small, fsdp_count):
    index = lax.axis_index("fsdp")
    step = 1
    while step < fsdp_count:
        ring = [(place, place ^ step) for place in range(fsdp_count)]
        side = (index // step) % 2
        value = value.reshape(fsdp_count // (2 * step), 2, -1, value.shape[-1])
        sent = lax.ppermute(
            lax.dynamic_index_in_dim(value, 1 - side, 1, keepdims=False), "fsdp", ring
        )
        kept = lax.dynamic_index_in_dim(value, side, 1, keepdims=False)
        value = kept.astype(jnp.float32) + sent.astype(jnp.float32)
        small = small + lax.ppermute(small, "fsdp", ring)
        step *= 2
        if step < fsdp_count:
            value = value.astype(jnp.bfloat16)
        value, small = lax.optimization_barrier((value, small))
    return value.reshape(-1, value.shape[-1]), small + swap(small)


def gathered(pieces):
    return lax.all_gather(jnp.concatenate(pieces, axis=1), "fsdp", axis=0, tiled=True)


def scattered(joined):
    return lax.psum_scatter(joined, "fsdp", scatter_dimension=0, tiled=True).astype(jnp.float32)


WINDOW = 208
WINDOW_STEP = 192
LANES = 128
FAR_BELOW = -1e30


def turned_product(left, right):
    return lax.dot_general(
        left, right, (((1,), (1,)), ((), ())), preferred_element_type=jnp.float32
    )


def plain_product(left, right):
    return jnp.dot(left, right, preferred_element_type=jnp.float32)


def window_masks(image):
    low = (SEQ - WINDOW_STEP) * image
    high = low + SEQ
    rows = lax.broadcasted_iota(jnp.int32, (WINDOW, 1), 0)
    columns = lax.broadcasted_iota(jnp.int32, (1, WINDOW), 1)
    return (rows >= low) & (rows < high), (columns >= low) & (columns < high)


def window_chances(query_head, key_pair, row_live, column_live, scale):
    scores = jnp.where(column_live, turned_product(query_head, key_pair) * scale, FAR_BELOW)
    expanded = jnp.exp(scores - jnp.max(scores, axis=-1, keepdims=True))
    total = jnp.sum(expanded, axis=-1, keepdims=True)
    return jnp.where(row_live, expanded / total, 0.0)


def attend_kernel(
    place_ref,
    hidden_own_ref,
    hidden_other_ref,
    weights_ref,
    bias_ref,
    qkv_ref,
    mixed_own_ref,
    mixed_other_ref,
    sent_ref,
    kept_ref,
    mixed_wide,
    wide,
):
    width = mixed_own_ref.shape[1]
    row_count = sent_ref.shape[0]
    scale = (D // HEADS) ** (-0.5)
    place = place_ref[0]
    other = pl.ds(pl.multiple_of((1 - place) * row_count, 8), row_count)
    own = pl.ds(pl.multiple_of(place * row_count, 8), row_count)
    for part in range(3):
        span = pl.ds(part * width, width)
        for rows, hidden_ref in ((own, hidden_own_ref), (other, hidden_other_ref)):
            product = plain_product(hidden_ref[...], weights_ref[:, span])
            if part != 1:
                product = product + bias_ref[pl.ds(part // 2, 1), :]
            wide[rows, span] = product
    qkv_ref[...] = wide[...].astype(jnp.bfloat16)
    mixed_wide[...] = jnp.zeros_like(mixed_wide)
    lane_low = lax.broadcasted_iota(jnp.int32, (1, LANES), 1) < D // HEADS

    def one_image(image, carry):
        window = pl.ds(pl.multiple_of(image * WINDOW_STEP, 16), WINDOW)
        row_live, column_live = window_masks(image)
        for pair in range(width // LANES):
            query_pair = qkv_ref[window, pl.ds(pair * LANES, LANES)]
            key_pair = qkv_ref[window, pl.ds(width + pair * LANES, LANES)]
            value_pair = qkv_ref[window, pl.ds(2 * width + pair * LANES, LANES)]
            sides = []
            for lane_mask in (lane_low, ~lane_low):
                chances = window_chances(
                    jnp.where(lane_mask, query_pair, jnp.zeros_like(query_pair)),
                    key_pair,
                    row_live,
                    column_live,
                    scale,
                )
                sides.append(plain_product(chances.astype(jnp.bfloat16), value_pair))
            mixed_wide[window, pl.ds(pair * LANES, LANES)] += jnp.where(
                lane_low, sides[0], sides[1]
            )
        return carry

    lax.fori_loop(0, IMG_DEV, one_image, 0)
    turned = weights_ref[:, 3 * width :]
    mixed_own = mixed_wide[own, :].astype(jnp.bfloat16)
    mixed_other = mixed_wide[other, :].astype(jnp.bfloat16)
    mixed_own_ref[...] = mixed_own
    mixed_other_ref[...] = mixed_other
    sent_ref[...] = turned_product(mixed_other, turned).astype(jnp.bfloat16)
    kept_ref[...] = turned_product(mixed_own, turned)


def attend_back_kernel(
    place_ref,
    branch_own_ref,
    branch_other_ref,
    qkv_ref,
    weights_ref,
    stacked_own_ref,
    stacked_other_ref,
    sent_ref,
    kept_ref,
    sums_ref,
    mixed_grad,
    wide,
):
    width = mixed_grad.shape[1]
    row_count = sent_ref.shape[0]
    scale = (D // HEADS) ** (-0.5)
    place = place_ref[0]
    other = pl.ds(pl.multiple_of((1 - place) * row_count, 8), row_count)
    own = pl.ds(pl.multiple_of(place * row_count, 8), row_count)
    turned = weights_ref[:, 3 * width :]
    wide[own, :width] = plain_product(branch_own_ref[...], turned)
    wide[other, :width] = plain_product(branch_other_ref[...], turned)
    mixed_grad[...] = wide[:, :width].astype(jnp.bfloat16)
    wide[...] = jnp.zeros_like(wide)
    lane_low = lax.broadcasted_iota(jnp.int32, (1, LANES), 1) < D // HEADS

    def one_image(image, carry):
        window = pl.ds(pl.multiple_of(image * WINDOW_STEP, 16), WINDOW)
        row_live, column_live = window_masks(image)
        for pair in range(width // LANES):
            query_pair = qkv_ref[window, pl.ds(pair * LANES, LANES)]
            key_pair = qkv_ref[window, pl.ds(width + pair * LANES, LANES)]
            value_pair = qkv_ref[window, pl.ds(2 * width + pair * LANES, LANES)]
            grad_pair = mixed_grad[window, pl.ds(pair * LANES, LANES)]
            sides = []
            for lane_mask in (lane_low, ~lane_low):
                chances = window_chances(
                    jnp.where(lane_mask, query_pair, jnp.zeros_like(query_pair)),
                    key_pair,
                    row_live,
                    column_live,
                    scale,
                )
                weight_grad = turned_product(
                    jnp.where(lane_mask, grad_pair, jnp.zeros_like(grad_pair)), value_pair
                )
                row_sum = jnp.sum(weight_grad * chances, axis=-1, keepdims=True)
                score_grad = (chances * (weight_grad - row_sum)).astype(jnp.bfloat16)
                sides.append(
                    (
                        plain_product(score_grad, key_pair) * scale,
                        row_product(score_grad, query_pair) * scale,
                        row_product(chances.astype(jnp.bfloat16), grad_pair),
                    )
                )
            for part in range(3):
                wide[window, pl.ds(part * width + pair * LANES, LANES)] += jnp.where(
                    lane_low, sides[0][part], sides[1][part]
                )
        return carry

    lax.fori_loop(0, IMG_DEV, one_image, 0)
    weight = weights_ref[:, : 3 * width]
    stacked_own = wide[own, :].astype(jnp.bfloat16)
    stacked_other = wide[other, :].astype(jnp.bfloat16)
    stacked_own_ref[...] = stacked_own
    stacked_other_ref[...] = stacked_other
    sums_ref[...] = jnp.sum(stacked_own.astype(jnp.float32), axis=0, keepdims=True) + jnp.sum(
        stacked_other.astype(jnp.float32), axis=0, keepdims=True
    )
    sent_ref[...] = turned_product(stacked_other, weight).astype(jnp.bfloat16)
    kept_ref[...] = turned_product(stacked_own, weight)


def add_partial(product, partial_ref, total):
    @pl.when(pl.program_id(0) == 0)
    def _():
        total[...] = product

    @pl.when(pl.program_id(0) > 0)
    def _():
        total[...] += product

    @pl.when(pl.program_id(0) == pl.num_programs(0) - 1)
    def _():
        partial_ref[...] = total[...].astype(partial_ref.dtype)


def mlp_kernel(hidden_ref, up_ref, turned_ref, bias_ref, act_ref, slope_ref, partial_ref, total):
    pre = plain_product(hidden_ref[...], up_ref[...]) + bias_ref[...]
    normal = 0.5 * (1.0 + lax.erf(pre * (0.5**0.5)))
    density = jnp.exp(-0.5 * pre * pre) * (0.5 / math.pi) ** 0.5
    active = (pre * normal).astype(jnp.bfloat16)
    act_ref[...] = active
    slope_ref[...] = (normal + pre * density).astype(jnp.bfloat16)
    add_partial(turned_product(active, turned_ref[...]), partial_ref, total)


def mlp_back_kernel(
    branch_ref, slope_ref, turned_ref, up_ref, pre_ref, sums_ref, partial_ref, total
):
    act_grad = plain_product(branch_ref[...], turned_ref[...])
    pre_grad = (act_grad * slope_ref[...].astype(jnp.float32)).astype(jnp.bfloat16)
    pre_ref[...] = pre_grad
    sums_ref[...] = jnp.sum(pre_grad.astype(jnp.float32), axis=0, keepdims=True)
    add_partial(turned_product(pre_grad, up_ref[...]), partial_ref, total)


def grads_kernel(*refs):
    first_left, first_right, second_left, second_right = (
        (refs[2 * pair], refs[2 * pair + 1]) for pair in range(4)
    )
    grad_ref = refs[-1]
    cut = first_right[0].shape[1]
    for span, lefts, rights in (
        (slice(0, cut), first_left, first_right),
        (slice(cut, None), second_left, second_right),
    ):
        grad_ref[:, span] = sum(
            row_product(left[...], right[...]) for left, right in zip(lefts, rights)
        ).astype(jnp.bfloat16)


ROOM = 60 * 1024 * 1024


def columns(array, width, place):
    return array, pl.BlockSpec((array.shape[0], width), lambda step: (0, place))


def stepped(array, width, place=0):
    return array, pl.BlockSpec((array.shape[0], width), lambda step: (0, place + step))


def run_stepped(kernel, steps, operands, moving, fixed, name):
    outs = [jax.ShapeDtypeStruct(shape, dtype) for shape, dtype in moving + [fixed]]
    specs = [
        pl.BlockSpec((shape[0], shape[1] // steps), lambda step: (0, step))
        for shape, dtype in moving
    ]
    specs.append(pl.BlockSpec(fixed[0], lambda step: (0, 0)))
    return pl.pallas_call(
        kernel,
        grid=(steps,),
        in_specs=[spec for array, spec in operands],
        out_specs=specs,
        out_shape=outs,
        scratch_shapes=[pltpu.VMEM(fixed[0], jnp.float32)],
        compiler_params=pltpu.CompilerParams(vmem_limit_bytes=ROOM),
        name=name,
    )(*[array for array, spec in operands])


def whole(array):
    return array, pl.BlockSpec(array.shape, lambda step: (0,) * array.ndim)


def scalar(array):
    return array, pl.BlockSpec(memory_space=pltpu.SMEM)


def run_kernel(kernel, operands, results, scratch=(), name=None, flops=0):
    outs = [jax.ShapeDtypeStruct(shape, dtype) for shape, dtype in results]
    return pl.pallas_call(
        kernel,
        grid=(1,),
        in_specs=[spec for array, spec in operands],
        out_specs=[pl.BlockSpec(shape, lambda step, rank=len(shape): (0,) * rank) for shape, dtype in results],
        out_shape=outs,
        scratch_shapes=list(scratch),
        compiler_params=pltpu.CompilerParams(vmem_limit_bytes=ROOM),
        cost_estimate=pl.CostEstimate(
            flops=flops,
            transcendentals=0,
            bytes_accessed=sum(math.prod(out.shape) * out.dtype.itemsize for out in outs),
        ),
        name=name,
    )(*[array for array, spec in operands])


def packed_grads(pairs, total, width, place, held=None):
    operands = [whole(part) for pair in pairs for part in pair]
    aliases = {}
    if held is not None:
        aliases = {len(operands): 0}
        operands.append((held, pl.BlockSpec(memory_space=pl.ANY)))
    return pl.pallas_call(
        grads_kernel,
        grid=(1,),
        in_specs=[spec for array, spec in operands],
        out_specs=pl.BlockSpec((D, width), lambda step: (0, place)),
        out_shape=jax.ShapeDtypeStruct((D, total), jnp.bfloat16),
        input_output_aliases=aliases,
        compiler_params=pltpu.CompilerParams(vmem_limit_bytes=ROOM),
        name="packed_grads",
    )(*[array for array, spec in operands])


def on_device(
    tokens,
    qkv_weight,
    out_weight,
    up_weight,
    down_weight,
    norm_gain,
    norm_shift,
    qv_bias,
    out_bias,
    up_bias,
    cotangent,
):
    tp_index = lax.axis_index("tp")
    tp_count = lax.axis_size("tp")
    fsdp_count = lax.axis_size("fsdp")
    row_count = tokens.shape[0]
    local_width = qkv_weight.shape[3]
    inner_width = up_weight.shape[2]
    piece_rows = qkv_weight.shape[1]
    all_rows = IMG_DEV * SEQ
    slot_rows = row_count * tp_count
    live = (tp_index * row_count + jnp.arange(row_count) < all_rows)[:, None]
    cut_qkv = 3 * local_width
    cut_out = cut_qkv + local_width

    place = jnp.reshape(tp_index, (1,)).astype(jnp.int32)
    bf16 = jnp.bfloat16
    f32 = jnp.float32

    def attn_pieces(layer_index):
        return [
            qkv_weight[layer_index].reshape(piece_rows, cut_qkv),
            out_weight[layer_index].T,
        ]

    def mlp_pieces(layer_index):
        return [up_weight[layer_index], down_weight[layer_index].T]

    steps = 3
    chunk = inner_width // steps
    joint = 2 * inner_width + cut_out
    sources = []
    for layer_index in range(LAYERS):
        full = gathered(mlp_pieces(layer_index) + attn_pieces(layer_index))
        sources.append(
            (columns(full, cut_out, 2), stepped(full, chunk, 0), stepped(full, chunk, steps))
        )

    def back_half(branch, slope, down_side, up_side, kind):
        pre_grad, sums, partial_sum = run_stepped(
            mlp_back_kernel,
            steps,
            [whole(branch), stepped(slope, chunk), down_side, up_side],
            [((row_count, inner_width), bf16), ((1, inner_width), f32)],
            ((row_count, D), kind),
            "mlp_back",
        )
        return pre_grad, partial_sum, sums

    grad = jnp.where(live, cotangent.astype(f32), 0.0)
    branch_own = grad.astype(bf16)
    stream = tokens.astype(jnp.float32)
    saved_values = []
    for layer_index in range(LAYERS):
        attn_side, up_side, down_side = sources[layer_index]
        local_qv = lax.dynamic_slice_in_dim(
            qv_bias[layer_index], tp_index * local_width, local_width, 1
        )
        local_up = lax.dynamic_slice_in_dim(
            up_bias[layer_index], tp_index * inner_width, inner_width, 0
        )[None]
        layer_input = stream
        own_hidden = norm_rows(
            stream, norm_gain[layer_index, 0], norm_shift[layer_index, 0]
        ).astype(bf16)
        other_hidden = swap(own_hidden)
        qkv, mixed_own, mixed_other, sent, kept = run_kernel(
            attend_kernel,
            [scalar(place), whole(own_hidden), whole(other_hidden), attn_side, whole(local_qv)],
            [
                ((slot_rows, cut_qkv), bf16),
                ((row_count, local_width), bf16),
                ((row_count, local_width), bf16),
                ((row_count, D), bf16),
                ((row_count, D), f32),
            ],
            [pltpu.VMEM((slot_rows, local_width), f32), pltpu.VMEM((slot_rows, cut_qkv), f32)],
            name="attend",
        )
        stream = stream + (kept + swap(sent).astype(f32)) + out_bias[layer_index, 0]
        middle = stream
        hidden_own = norm_rows(
            stream, norm_gain[layer_index, 1], norm_shift[layer_index, 1]
        ).astype(bf16)
        hidden_other = swap(hidden_own)

        def mlp_half(hidden_half, kind):
            return run_stepped(
                mlp_kernel,
                steps,
                [whole(hidden_half), up_side, down_side, stepped(local_up, chunk)],
                [((row_count, inner_width), bf16), ((row_count, inner_width), bf16)],
                ((row_count, D), kind),
                "mlp",
            )

        act_own, slope_own, kept = mlp_half(hidden_own, f32)
        if layer_index < LAYERS - 1:
            hidden_other, kept = lax.optimization_barrier((hidden_other, kept))
        else:
            pre_own, kept_back, up_sums_own = back_half(
                branch_own, slope_own, down_side, up_side, f32
            )
            hidden_other, kept, kept_back = lax.optimization_barrier(
                (hidden_other, kept, kept_back)
            )
        act_other, slope_other, sent = mlp_half(hidden_other, bf16)
        if layer_index < LAYERS - 1:
            stream = stream + (kept + swap(sent).astype(f32)) + out_bias[layer_index, 1]
        else:
            last_sent, last_kept = sent, kept
        saved_values.append(
            (
                layer_input,
                middle,
                (own_hidden, other_hidden),
                qkv,
                (mixed_own, mixed_other),
                hidden_own,
                hidden_other,
                slope_own,
                slope_other,
                act_own,
                act_other,
                (attn_side, up_side, down_side),
            )
        )
    held = None
    scattered_grads = []
    gain_grads = [None] * LAYERS
    shift_grads = [None] * LAYERS
    qv_grads = [None] * LAYERS
    out_bias_grads = [None] * LAYERS
    up_bias_grads = [None] * LAYERS
    for layer_index in reversed(range(LAYERS)):
        (
            layer_input,
            middle,
            hidden_pair,
            qkv,
            mixed_pair,
            hidden_own,
            hidden_other,
            slope_own,
            slope_other,
            act_own,
            act_other,
            (attn_side, up_side, down_side),
        ) = saved_values[layer_index]
        branch_other = swap(branch_own)
        down_bias_grad = jnp.sum(branch_own.astype(f32), axis=0)
        if layer_index < LAYERS - 1:
            pre_own, kept_back, up_sums_own = back_half(
                branch_own, slope_own, down_side, up_side, f32
            )
            branch_other, kept_back = lax.optimization_barrier((branch_other, kept_back))
        pre_other, sent, up_sums_other = back_half(
            branch_other, slope_other, down_side, up_side, bf16
        )
        up_vector_grad = (up_sums_own + up_sums_other)[0]
        mlp_grad = packed_grads(
            [
                (hidden_own, hidden_other),
                (pre_own, pre_other),
                (branch_own, branch_other),
                (act_own, act_other),
            ],
            2 * inner_width if held is None else joint,
            2 * inner_width,
            0,
            held,
        )
        received, mlp_grad = lax.optimization_barrier((swap(sent), mlp_grad))
        norm_grad = kept_back + received.astype(f32)
        scattered_grads.append(scattered(mlp_grad))
        norm_back = jax.vjp(
            norm_rows, middle, norm_gain[layer_index, 1], norm_shift[layer_index, 1]
        )[1]
        middle_grad, gain_two, shift_two = norm_back(norm_grad)
        grad = grad + middle_grad
        branch_own = grad.astype(bf16)
        attn_bias_grad = jnp.sum(branch_own.astype(f32), axis=0)
        branch_other = swap(branch_own)
        if layer_index == LAYERS - 1:
            branch_other, last_sent = lax.optimization_barrier((branch_other, last_sent))
            last_received = swap(last_sent)
        stacked_own, stacked_other, sent, kept, stacked_sums = run_kernel(
            attend_back_kernel,
            [scalar(place), whole(branch_own), whole(branch_other), whole(qkv), attn_side],
            [
                ((row_count, cut_qkv), bf16),
                ((row_count, cut_qkv), bf16),
                ((row_count, D), bf16),
                ((row_count, D), f32),
                ((1, cut_qkv), f32),
            ],
            [pltpu.VMEM((slot_rows, local_width), bf16), pltpu.VMEM((slot_rows, cut_qkv), f32)],
            name="attend_back",
        )
        stacked_sums = stacked_sums.reshape(3, local_width)
        attn_grad = packed_grads(
            [hidden_pair, (stacked_own, stacked_other), (branch_own, branch_other), mixed_pair],
            joint if layer_index else cut_out,
            cut_out,
            2 if layer_index else 0,
        )
        if layer_index == LAYERS - 1:
            sent, last_received = lax.optimization_barrier((sent, last_received))
            stream = stream + (last_kept + last_received.astype(f32)) + out_bias[layer_index, 1]
            activations = jnp.where(live, stream, 0.0).astype(bf16)
        received, attn_grad = lax.optimization_barrier((swap(sent), attn_grad))
        norm_grad = kept + received.astype(f32)
        held = attn_grad
        norm_back = jax.vjp(
            norm_rows, layer_input, norm_gain[layer_index, 0], norm_shift[layer_index, 0]
        )[1]
        input_part, gain_one, shift_one = norm_back(norm_grad)
        grad = grad + input_part
        branch_own = grad.astype(bf16)
        gain_grads[layer_index] = jnp.stack([gain_one, gain_two])
        shift_grads[layer_index] = jnp.stack([shift_one, shift_two])
        qv_local = jnp.stack([stacked_sums[0], stacked_sums[2]])
        qv_grads[layer_index] = lax.dynamic_update_slice_in_dim(
            jnp.zeros((2, D), jnp.float32), qv_local, tp_index * local_width, 1
        )
        out_bias_grads[layer_index] = jnp.stack([attn_bias_grad, down_bias_grad])
        up_bias_grads[layer_index] = lax.dynamic_update_slice_in_dim(
            jnp.zeros((FF,), jnp.float32), up_vector_grad, tp_index * inner_width, 0
        ).reshape(FF // D, D)
    small = jnp.concatenate(
        gain_grads + shift_grads + qv_grads + out_bias_grads + up_bias_grads, axis=0
    )
    attn_first, small = reduced_together(held, small, fsdp_count)
    pair = 2 * LAYERS
    small_totals = [small[pair * k : pair * (k + 1)].reshape(LAYERS, 2, D) for k in range(4)]
    up_totals = small[4 * pair :].reshape(LAYERS, FF)
    mlp_last, joint_owned = scattered_grads
    owned = [
        (joint_owned[:, : 2 * inner_width], attn_first),
        (mlp_last, joint_owned[:, 2 * inner_width :]),
    ]
    up_all = jnp.stack([mlp[:, :inner_width] for mlp, attn in owned])
    down_all = jnp.stack([mlp[:, inner_width:].T for mlp, attn in owned])
    qkv_all = jnp.stack(
        [attn[:, :cut_qkv].reshape(piece_rows, 3, local_width) for mlp, attn in owned]
    )
    out_all = jnp.stack([attn[:, cut_qkv:].T for mlp, attn in owned])
    input_grad = jnp.where(live, grad, 0.0)
    return (
        activations,
        input_grad,
        qkv_all,
        out_all,
        up_all,
        down_all,
        small_totals[0],
        small_totals[1],
        small_totals[2],
        small_totals[3],
        up_totals,
    )


def solution(mesh):
    return jax.shard_map(
        on_device,
        mesh=mesh,
        in_specs=(
            P(("fsdp", "tp"), None),
            P(None, "fsdp", None, "tp"),
            P(None, "tp", "fsdp"),
            P(None, "fsdp", "tp"),
            P(None, "tp", "fsdp"),
            P(),
            P(),
            P(),
            P(),
            P(),
            P(("fsdp", "tp"), None),
        ),
        out_specs=(
            P(("fsdp", "tp"), None),
            P(("fsdp", "tp"), None),
            P(None, "fsdp", None, "tp"),
            P(None, "tp", "fsdp"),
            P(None, "fsdp", "tp"),
            P(None, "tp", "fsdp"),
            P(),
            P(),
            P(),
            P(),
            P(),
        ),
        check_vma=False,
    )
```

```python
import math

import jax
import jax.numpy as jnp
from jax import lax
from jax.experimental import pallas as pl
from jax.experimental.pallas import tpu as pltpu
from jax.sharding import PartitionSpec as P

D = 768
HEADS = 12
FF = 3072
SEQ = 197
LAYERS = 2
IMG_DEV = 3


def norm_rows(value, gain_vector, shift_vector):
    row_mean = jnp.mean(value, axis=-1, keepdims=True)
    centred = value - row_mean
    row_var = jnp.mean(centred * centred, axis=-1, keepdims=True)
    return centred * lax.rsqrt(row_var + 1e-06) * gain_vector + shift_vector


def row_product(left, right):
    return lax.dot_general(
        left, right, (((0,), (0,)), ((), ())), preferred_element_type=jnp.float32
    )


def swap(value):
    return lax.ppermute(value, "tp", [(0, 1), (1, 0)])


def reduced_together(value, small, fsdp_count):
    index = lax.axis_index("fsdp")
    step = 1
    while step < fsdp_count:
        ring = [(place, place ^ step) for place in range(fsdp_count)]
        side = (index // step) % 2
        value = value.reshape(fsdp_count // (2 * step), 2, -1, value.shape[-1])
        sent = lax.ppermute(
            lax.dynamic_index_in_dim(value, 1 - side, 1, keepdims=False), "fsdp", ring
        )
        kept = lax.dynamic_index_in_dim(value, side, 1, keepdims=False)
        value = kept.astype(jnp.float32) + sent.astype(jnp.float32)
        small = small + lax.ppermute(small, "fsdp", ring)
        step *= 2
        if step < fsdp_count:
            value = value.astype(jnp.bfloat16)
        value, small = lax.optimization_barrier((value, small))
    return value.reshape(-1, value.shape[-1]), small + swap(small)


def gathered(pieces):
    return lax.all_gather(jnp.concatenate(pieces, axis=1), "fsdp", axis=0, tiled=True)


def scattered(joined):
    return lax.psum_scatter(joined, "fsdp", scatter_dimension=0, tiled=True).astype(jnp.float32)


WINDOW = 208
WINDOW_STEP = 192
LANES = 128
FAR_BELOW = -1e30


def turned_product(left, right):
    return lax.dot_general(
        left, right, (((1,), (1,)), ((), ())), preferred_element_type=jnp.float32
    )


def plain_product(left, right):
    return jnp.dot(left, right, preferred_element_type=jnp.float32)


def window_masks(image):
    low = (SEQ - WINDOW_STEP) * image
    high = low + SEQ
    rows = lax.broadcasted_iota(jnp.int32, (WINDOW, 1), 0)
    columns = lax.broadcasted_iota(jnp.int32, (1, WINDOW), 1)
    return (rows >= low) & (rows < high), (columns >= low) & (columns < high)


def window_chances(query_head, key_pair, row_live, column_live, scale):
    scores = jnp.where(column_live, turned_product(query_head, key_pair) * scale, FAR_BELOW)
    expanded = jnp.exp(scores - jnp.max(scores, axis=-1, keepdims=True))
    total = jnp.sum(expanded, axis=-1, keepdims=True)
    return jnp.where(row_live, expanded / total, 0.0)


def attend_kernel(
    place_ref,
    hidden_own_ref,
    hidden_other_ref,
    weights_ref,
    bias_ref,
    qkv_ref,
    mixed_own_ref,
    mixed_other_ref,
    sent_ref,
    kept_ref,
    mixed_wide,
    wide,
):
    width = mixed_own_ref.shape[1]
    row_count = sent_ref.shape[0]
    scale = (D // HEADS) ** (-0.5)
    place = place_ref[0]
    other = pl.ds(pl.multiple_of((1 - place) * row_count, 8), row_count)
    own = pl.ds(pl.multiple_of(place * row_count, 8), row_count)
    for part in range(3):
        span = pl.ds(part * width, width)
        for rows, hidden_ref in ((own, hidden_own_ref), (other, hidden_other_ref)):
            product = plain_product(hidden_ref[...], weights_ref[:, span])
            if part != 1:
                product = product + bias_ref[pl.ds(part // 2, 1), :]
            wide[rows, span] = product
    qkv_ref[...] = wide[...].astype(jnp.bfloat16)
    mixed_wide[...] = jnp.zeros_like(mixed_wide)
    lane_low = lax.broadcasted_iota(jnp.int32, (1, LANES), 1) < D // HEADS

    def one_image(image):
        window = pl.ds(image * WINDOW_STEP, WINDOW)
        row_live, column_live = window_masks(image)
        for pair in range(width // LANES):
            query_pair = qkv_ref[window, pl.ds(pair * LANES, LANES)]
            key_pair = qkv_ref[window, pl.ds(width + pair * LANES, LANES)]
            value_pair = qkv_ref[window, pl.ds(2 * width + pair * LANES, LANES)]
            sides = []
            for lane_mask in (lane_low, ~lane_low):
                chances = window_chances(
                    jnp.where(lane_mask, query_pair, jnp.zeros_like(query_pair)),
                    key_pair,
                    row_live,
                    column_live,
                    scale,
                )
                sides.append(plain_product(chances.astype(jnp.bfloat16), value_pair))
            mixed_wide[window, pl.ds(pair * LANES, LANES)] += jnp.where(
                lane_low, sides[0], sides[1]
            )

    for image in range(IMG_DEV):
        one_image(image)
    turned = weights_ref[:, 3 * width :]
    mixed_own = mixed_wide[own, :].astype(jnp.bfloat16)
    mixed_other = mixed_wide[other, :].astype(jnp.bfloat16)
    mixed_own_ref[...] = mixed_own
    mixed_other_ref[...] = mixed_other
    sent_ref[...] = turned_product(mixed_other, turned).astype(jnp.bfloat16)
    kept_ref[...] = turned_product(mixed_own, turned)


def attend_back_kernel(
    place_ref,
    branch_own_ref,
    branch_other_ref,
    qkv_ref,
    weights_ref,
    stacked_own_ref,
    stacked_other_ref,
    sent_ref,
    kept_ref,
    sums_ref,
    mixed_grad,
    wide,
):
    width = mixed_grad.shape[1]
    row_count = sent_ref.shape[0]
    scale = (D // HEADS) ** (-0.5)
    place = place_ref[0]
    other = pl.ds(pl.multiple_of((1 - place) * row_count, 8), row_count)
    own = pl.ds(pl.multiple_of(place * row_count, 8), row_count)
    turned = weights_ref[:, 3 * width :]
    wide[own, :width] = plain_product(branch_own_ref[...], turned)
    wide[other, :width] = plain_product(branch_other_ref[...], turned)
    mixed_grad[...] = wide[:, :width].astype(jnp.bfloat16)
    wide[...] = jnp.zeros_like(wide)
    lane_low = lax.broadcasted_iota(jnp.int32, (1, LANES), 1) < D // HEADS

    def one_image(image):
        window = pl.ds(image * WINDOW_STEP, WINDOW)
        row_live, column_live = window_masks(image)
        for pair in range(width // LANES):
            query_pair = qkv_ref[window, pl.ds(pair * LANES, LANES)]
            key_pair = qkv_ref[window, pl.ds(width + pair * LANES, LANES)]
            value_pair = qkv_ref[window, pl.ds(2 * width + pair * LANES, LANES)]
            grad_pair = mixed_grad[window, pl.ds(pair * LANES, LANES)]
            sides = []
            for lane_mask in (lane_low, ~lane_low):
                chances = window_chances(
                    jnp.where(lane_mask, query_pair, jnp.zeros_like(query_pair)),
                    key_pair,
                    row_live,
                    column_live,
                    scale,
                )
                weight_grad = turned_product(
                    jnp.where(lane_mask, grad_pair, jnp.zeros_like(grad_pair)), value_pair
                )
                row_sum = jnp.sum(weight_grad * chances, axis=-1, keepdims=True)
                score_grad = (chances * (weight_grad - row_sum)).astype(jnp.bfloat16)
                sides.append(
                    (
                        plain_product(score_grad, key_pair) * scale,
                        row_product(score_grad, query_pair) * scale,
                        row_product(chances.astype(jnp.bfloat16), grad_pair),
                    )
                )
            for part in range(3):
                wide[window, pl.ds(part * width + pair * LANES, LANES)] += jnp.where(
                    lane_low, sides[0][part], sides[1][part]
                )

    for image in range(IMG_DEV):
        one_image(image)
    weight = weights_ref[:, : 3 * width]
    stacked_own = wide[own, :].astype(jnp.bfloat16)
    stacked_other = wide[other, :].astype(jnp.bfloat16)
    stacked_own_ref[...] = stacked_own
    stacked_other_ref[...] = stacked_other
    sums_ref[...] = jnp.sum(stacked_own.astype(jnp.float32), axis=0, keepdims=True) + jnp.sum(
        stacked_other.astype(jnp.float32), axis=0, keepdims=True
    )
    sent_ref[...] = turned_product(stacked_other, weight).astype(jnp.bfloat16)
    kept_ref[...] = turned_product(stacked_own, weight)


def mlp_kernel(hidden_ref, up_ref, turned_ref, bias_ref, act_ref, slope_ref, partial_ref):
    pre = plain_product(hidden_ref[...], up_ref[...]) + bias_ref[...]
    normal = 0.5 * (1.0 + lax.erf(pre * (0.5**0.5)))
    density = jnp.exp(-0.5 * pre * pre) * (0.5 / math.pi) ** 0.5
    active = (pre * normal).astype(jnp.bfloat16)
    act_ref[...] = active
    slope_ref[...] = (normal + pre * density).astype(jnp.bfloat16)
    partial_ref[...] = turned_product(active, turned_ref[...]).astype(partial_ref.dtype)


def mlp_back_kernel(branch_ref, slope_ref, turned_ref, up_ref, pre_ref, sums_ref, partial_ref):
    act_grad = plain_product(branch_ref[...], turned_ref[...])
    pre_grad = (act_grad * slope_ref[...].astype(jnp.float32)).astype(jnp.bfloat16)
    pre_ref[...] = pre_grad
    sums_ref[...] = jnp.sum(pre_grad.astype(jnp.float32), axis=0, keepdims=True)
    partial_ref[...] = turned_product(pre_grad, up_ref[...]).astype(partial_ref.dtype)


def grads_kernel(*refs):
    first_left, first_right, second_left, second_right = (
        (refs[2 * pair], refs[2 * pair + 1]) for pair in range(4)
    )
    grad_ref = refs[-1]
    cut = first_right[0].shape[1]
    for span, lefts, rights in (
        (slice(0, cut), first_left, first_right),
        (slice(cut, None), second_left, second_right),
    ):
        grad_ref[:, span] = sum(
            row_product(left[...], right[...]) for left, right in zip(lefts, rights)
        ).astype(jnp.bfloat16)


ROOM = 60 * 1024 * 1024


def columns(array, width, place):
    return array, pl.BlockSpec((array.shape[0], width), lambda step: (0, place))


def whole(array):
    return array, pl.BlockSpec(array.shape, lambda step: (0,) * array.ndim)


def scalar(array):
    return array, pl.BlockSpec(memory_space=pltpu.SMEM)


def run_kernel(kernel, operands, results, scratch=(), name=None, flops=0):
    outs = [jax.ShapeDtypeStruct(shape, dtype) for shape, dtype in results]
    return pl.pallas_call(
        kernel,
        grid=(1,),
        in_specs=[spec for array, spec in operands],
        out_specs=[pl.BlockSpec(shape, lambda step, rank=len(shape): (0,) * rank) for shape, dtype in results],
        out_shape=outs,
        scratch_shapes=list(scratch),
        compiler_params=pltpu.CompilerParams(vmem_limit_bytes=ROOM),
        cost_estimate=pl.CostEstimate(
            flops=flops,
            transcendentals=0,
            bytes_accessed=sum(math.prod(out.shape) * out.dtype.itemsize for out in outs),
        ),
        name=name,
    )(*[array for array, spec in operands])


def packed_grads(pairs, total, width, place, held=None):
    operands = [whole(part) for pair in pairs for part in pair]
    aliases = {}
    if held is not None:
        aliases = {len(operands): 0}
        operands.append((held, pl.BlockSpec(memory_space=pl.ANY)))
    return pl.pallas_call(
        grads_kernel,
        grid=(1,),
        in_specs=[spec for array, spec in operands],
        out_specs=pl.BlockSpec((D, width), lambda step: (0, place)),
        out_shape=jax.ShapeDtypeStruct((D, total), jnp.bfloat16),
        input_output_aliases=aliases,
        compiler_params=pltpu.CompilerParams(vmem_limit_bytes=ROOM),
        name="packed_grads",
    )(*[array for array, spec in operands])


def on_device(
    tokens,
    qkv_weight,
    out_weight,
    up_weight,
    down_weight,
    norm_gain,
    norm_shift,
    qv_bias,
    out_bias,
    up_bias,
    cotangent,
):
    tp_index = lax.axis_index("tp")
    tp_count = lax.axis_size("tp")
    fsdp_count = lax.axis_size("fsdp")
    row_count = tokens.shape[0]
    local_width = qkv_weight.shape[3]
    inner_width = up_weight.shape[2]
    piece_rows = qkv_weight.shape[1]
    all_rows = IMG_DEV * SEQ
    slot_rows = row_count * tp_count
    live = (tp_index * row_count + jnp.arange(row_count) < all_rows)[:, None]
    cut_qkv = 3 * local_width
    cut_out = cut_qkv + local_width

    place = jnp.reshape(tp_index, (1,)).astype(jnp.int32)
    bf16 = jnp.bfloat16
    f32 = jnp.float32

    def attn_pieces(layer_index):
        return [
            qkv_weight[layer_index].reshape(piece_rows, cut_qkv),
            out_weight[layer_index].T,
        ]

    def mlp_pieces(layer_index):
        return [up_weight[layer_index], down_weight[layer_index].T]

    joint = 2 * inner_width + cut_out
    sources = []
    for layer_index in range(LAYERS):
        full = gathered(mlp_pieces(layer_index) + attn_pieces(layer_index))
        sources.append(
            (columns(full, cut_out, 2), columns(full, inner_width, 0), columns(full, inner_width, 1))
        )

    def back_half(branch, slope, down_side, up_side, kind):
        pre_grad, sums, partial_sum = run_kernel(
            mlp_back_kernel,
            [whole(branch), whole(slope), down_side, up_side],
            [((row_count, inner_width), bf16), ((1, inner_width), f32), ((row_count, D), kind)],
            name="mlp_back",
        )
        return pre_grad, partial_sum, sums

    grad = jnp.where(live, cotangent.astype(f32), 0.0)
    branch_own = grad.astype(bf16)
    stream = tokens.astype(jnp.float32)
    saved_values = []
    for layer_index in range(LAYERS):
        attn_side, up_side, down_side = sources[layer_index]
        local_qv = lax.dynamic_slice_in_dim(
            qv_bias[layer_index], tp_index * local_width, local_width, 1
        )
        local_up = lax.dynamic_slice_in_dim(
            up_bias[layer_index], tp_index * inner_width, inner_width, 0
        )[None]
        layer_input = stream
        own_hidden = norm_rows(
            stream, norm_gain[layer_index, 0], norm_shift[layer_index, 0]
        ).astype(bf16)
        other_hidden = swap(own_hidden)
        qkv, mixed_own, mixed_other, sent, kept = run_kernel(
            attend_kernel,
            [scalar(place), whole(own_hidden), whole(other_hidden), attn_side, whole(local_qv)],
            [
                ((slot_rows, cut_qkv), bf16),
                ((row_count, local_width), bf16),
                ((row_count, local_width), bf16),
                ((row_count, D), bf16),
                ((row_count, D), f32),
            ],
            [pltpu.VMEM((slot_rows, local_width), f32), pltpu.VMEM((slot_rows, cut_qkv), f32)],
            name="attend",
        )
        stream = stream + (kept + swap(sent).astype(f32)) + out_bias[layer_index, 0]
        middle = stream
        hidden_own = norm_rows(
            stream, norm_gain[layer_index, 1], norm_shift[layer_index, 1]
        ).astype(bf16)
        hidden_other = swap(hidden_own)

        def mlp_half(hidden_half, kind):
            return run_kernel(
                mlp_kernel,
                [whole(hidden_half), up_side, down_side, whole(local_up)],
                [
                    ((row_count, inner_width), bf16),
                    ((row_count, inner_width), bf16),
                    ((row_count, D), kind),
                ],
                name="mlp",
            )

        act_own, slope_own, kept = mlp_half(hidden_own, f32)
        if layer_index < LAYERS - 1:
            hidden_other, kept = lax.optimization_barrier((hidden_other, kept))
        else:
            pre_own, kept_back, up_sums_own = back_half(
                branch_own, slope_own, down_side, up_side, f32
            )
            hidden_other, kept, kept_back = lax.optimization_barrier(
                (hidden_other, kept, kept_back)
            )
        act_other, slope_other, sent = mlp_half(hidden_other, bf16)
        if layer_index < LAYERS - 1:
            stream = stream + (kept + swap(sent).astype(f32)) + out_bias[layer_index, 1]
        else:
            last_sent, last_kept = sent, kept
        saved_values.append(
            (
                layer_input,
                middle,
                (own_hidden, other_hidden),
                qkv,
                (mixed_own, mixed_other),
                hidden_own,
                hidden_other,
                slope_own,
                slope_other,
                act_own,
                act_other,
                (attn_side, up_side, down_side),
            )
        )
    held = None
    scattered_grads = []
    gain_grads = [None] * LAYERS
    shift_grads = [None] * LAYERS
    qv_grads = [None] * LAYERS
    out_bias_grads = [None] * LAYERS
    up_bias_grads = [None] * LAYERS
    for layer_index in reversed(range(LAYERS)):
        (
            layer_input,
            middle,
            hidden_pair,
            qkv,
            mixed_pair,
            hidden_own,
            hidden_other,
            slope_own,
            slope_other,
            act_own,
            act_other,
            (attn_side, up_side, down_side),
        ) = saved_values[layer_index]
        branch_other = swap(branch_own)
        down_bias_grad = jnp.sum(branch_own.astype(f32), axis=0)
        if layer_index < LAYERS - 1:
            pre_own, kept_back, up_sums_own = back_half(
                branch_own, slope_own, down_side, up_side, f32
            )
            branch_other, kept_back = lax.optimization_barrier((branch_other, kept_back))
        pre_other, sent, up_sums_other = back_half(
            branch_other, slope_other, down_side, up_side, bf16
        )
        up_vector_grad = (up_sums_own + up_sums_other)[0]
        mlp_grad = packed_grads(
            [
                (hidden_own, hidden_other),
                (pre_own, pre_other),
                (branch_own, branch_other),
                (act_own, act_other),
            ],
            2 * inner_width if held is None else joint,
            2 * inner_width,
            0,
            held,
        )
        received, mlp_grad = lax.optimization_barrier((swap(sent), mlp_grad))
        norm_grad = kept_back + received.astype(f32)
        scattered_grads.append(scattered(mlp_grad))
        norm_back = jax.vjp(
            norm_rows, middle, norm_gain[layer_index, 1], norm_shift[layer_index, 1]
        )[1]
        middle_grad, gain_two, shift_two = norm_back(norm_grad)
        grad = grad + middle_grad
        branch_own = grad.astype(bf16)
        attn_bias_grad = jnp.sum(branch_own.astype(f32), axis=0)
        branch_other = swap(branch_own)
        if layer_index == LAYERS - 1:
            branch_other, last_sent = lax.optimization_barrier((branch_other, last_sent))
            last_received = swap(last_sent)
        stacked_own, stacked_other, sent, kept, stacked_sums = run_kernel(
            attend_back_kernel,
            [scalar(place), whole(branch_own), whole(branch_other), whole(qkv), attn_side],
            [
                ((row_count, cut_qkv), bf16),
                ((row_count, cut_qkv), bf16),
                ((row_count, D), bf16),
                ((row_count, D), f32),
                ((1, cut_qkv), f32),
            ],
            [pltpu.VMEM((slot_rows, local_width), bf16), pltpu.VMEM((slot_rows, cut_qkv), f32)],
            name="attend_back",
        )
        stacked_sums = stacked_sums.reshape(3, local_width)
        attn_grad = packed_grads(
            [hidden_pair, (stacked_own, stacked_other), (branch_own, branch_other), mixed_pair],
            joint if layer_index else cut_out,
            cut_out,
            2 if layer_index else 0,
        )
        if layer_index == LAYERS - 1:
            sent, last_received = lax.optimization_barrier((sent, last_received))
            stream = stream + (last_kept + last_received.astype(f32)) + out_bias[layer_index, 1]
            activations = jnp.where(live, stream, 0.0).astype(bf16)
        received, attn_grad = lax.optimization_barrier((swap(sent), attn_grad))
        norm_grad = kept + received.astype(f32)
        held = attn_grad
        norm_back = jax.vjp(
            norm_rows, layer_input, norm_gain[layer_index, 0], norm_shift[layer_index, 0]
        )[1]
        input_part, gain_one, shift_one = norm_back(norm_grad)
        grad = grad + input_part
        branch_own = grad.astype(bf16)
        gain_grads[layer_index] = jnp.stack([gain_one, gain_two])
        shift_grads[layer_index] = jnp.stack([shift_one, shift_two])
        qv_local = jnp.stack([stacked_sums[0], stacked_sums[2]])
        qv_grads[layer_index] = lax.dynamic_update_slice_in_dim(
            jnp.zeros((2, D), jnp.float32), qv_local, tp_index * local_width, 1
        )
        out_bias_grads[layer_index] = jnp.stack([attn_bias_grad, down_bias_grad])
        up_bias_grads[layer_index] = lax.dynamic_update_slice_in_dim(
            jnp.zeros((FF,), jnp.float32), up_vector_grad, tp_index * inner_width, 0
        ).reshape(FF // D, D)
    small = jnp.concatenate(
        gain_grads + shift_grads + qv_grads + out_bias_grads + up_bias_grads, axis=0
    )
    attn_first, small = reduced_together(held, small, fsdp_count)
    pair = 2 * LAYERS
    small_totals = [small[pair * k : pair * (k + 1)].reshape(LAYERS, 2, D) for k in range(4)]
    up_totals = small[4 * pair :].reshape(LAYERS, FF)
    mlp_last, joint_owned = scattered_grads
    owned = [
        (joint_owned[:, : 2 * inner_width], attn_first),
        (mlp_last, joint_owned[:, 2 * inner_width :]),
    ]
    up_all = jnp.stack([mlp[:, :inner_width] for mlp, attn in owned])
    down_all = jnp.stack([mlp[:, inner_width:].T for mlp, attn in owned])
    qkv_all = jnp.stack(
        [attn[:, :cut_qkv].reshape(piece_rows, 3, local_width) for mlp, attn in owned]
    )
    out_all = jnp.stack([attn[:, cut_qkv:].T for mlp, attn in owned])
    input_grad = jnp.where(live, grad, 0.0)
    return (
        activations,
        input_grad,
        qkv_all,
        out_all,
        up_all,
        down_all,
        small_totals[0],
        small_totals[1],
        small_totals[2],
        small_totals[3],
        up_totals,
    )


def solution(mesh):
    return jax.shard_map(
        on_device,
        mesh=mesh,
        in_specs=(
            P(("fsdp", "tp"), None),
            P(None, "fsdp", None, "tp"),
            P(None, "tp", "fsdp"),
            P(None, "fsdp", "tp"),
            P(None, "tp", "fsdp"),
            P(),
            P(),
            P(),
            P(),
            P(),
            P(("fsdp", "tp"), None),
        ),
        out_specs=(
            P(("fsdp", "tp"), None),
            P(("fsdp", "tp"), None),
            P(None, "fsdp", None, "tp"),
            P(None, "tp", "fsdp"),
            P(None, "fsdp", "tp"),
            P(None, "tp", "fsdp"),
            P(),
            P(),
            P(),
            P(),
            P(),
        ),
        check_vma=False,
    )
```

```python
import math

import jax
import jax.numpy as jnp
from jax import lax
from jax.experimental import pallas as pl
from jax.experimental.pallas import tpu as pltpu
from jax.sharding import PartitionSpec as P

D = 768
HEADS = 12
FF = 3072
SEQ = 197
LAYERS = 2
IMG_DEV = 3


def norm_rows(value, gain_vector, shift_vector):
    row_mean = jnp.mean(value, axis=-1, keepdims=True)
    centred = value - row_mean
    row_var = jnp.mean(centred * centred, axis=-1, keepdims=True)
    return centred * lax.rsqrt(row_var + 1e-06) * gain_vector + shift_vector


def row_product(left, right):
    return lax.dot_general(
        left, right, (((0,), (0,)), ((), ())), preferred_element_type=jnp.float32
    )


def swap(value):
    return lax.ppermute(value, "tp", [(0, 1), (1, 0)])


def reduced_together(value, small, fsdp_count):
    index = lax.axis_index("fsdp")
    step = 1
    while step < fsdp_count:
        ring = [(place, place ^ step) for place in range(fsdp_count)]
        side = (index // step) % 2
        value = value.reshape(fsdp_count // (2 * step), 2, -1, value.shape[-1])
        sent = lax.ppermute(
            lax.dynamic_index_in_dim(value, 1 - side, 1, keepdims=False), "fsdp", ring
        )
        kept = lax.dynamic_index_in_dim(value, side, 1, keepdims=False)
        value = kept.astype(jnp.float32) + sent.astype(jnp.float32)
        small = small + lax.ppermute(small, "fsdp", ring)
        step *= 2
        if step < fsdp_count:
            value = value.astype(jnp.bfloat16)
        value, small = lax.optimization_barrier((value, small))
    return value.reshape(-1, value.shape[-1]), small + swap(small)


def gathered(pieces):
    return lax.all_gather(jnp.concatenate(pieces, axis=1), "fsdp", axis=0, tiled=True)


def scattered(joined):
    return lax.psum_scatter(joined, "fsdp", scatter_dimension=0, tiled=True).astype(jnp.float32)


WINDOW = 208
WINDOW_STEP = 192
LANES = 128
GRAD_ROWS = 256
FAR_BELOW = -1e30


def turned_product(left, right):
    return lax.dot_general(
        left, right, (((1,), (1,)), ((), ())), preferred_element_type=jnp.float32
    )


def plain_product(left, right):
    return jnp.dot(left, right, preferred_element_type=jnp.float32)


def window_masks(image):
    low = (SEQ - WINDOW_STEP) * image
    high = low + SEQ
    rows = lax.broadcasted_iota(jnp.int32, (WINDOW, 1), 0)
    columns = lax.broadcasted_iota(jnp.int32, (1, WINDOW), 1)
    return (rows >= low) & (rows < high), (columns >= low) & (columns < high)


def window_chances(query_head, key_pair, row_live, column_live, scale):
    scores = jnp.where(column_live, turned_product(query_head, key_pair) * scale, FAR_BELOW)
    expanded = jnp.exp(scores - jnp.max(scores, axis=-1, keepdims=True))
    total = jnp.sum(expanded, axis=-1, keepdims=True)
    return jnp.where(row_live, expanded / total, 0.0)


def attend_kernel(
    place_ref,
    hidden_own_ref,
    hidden_other_ref,
    weights_ref,
    bias_ref,
    qkv_ref,
    mixed_own_ref,
    mixed_other_ref,
    sent_ref,
    kept_ref,
    mixed_wide,
    wide,
):
    width = mixed_own_ref.shape[1]
    row_count = sent_ref.shape[0]
    scale = (D // HEADS) ** (-0.5)
    place = place_ref[0]
    other = pl.ds(pl.multiple_of((1 - place) * row_count, 8), row_count)
    own = pl.ds(pl.multiple_of(place * row_count, 8), row_count)
    for part in range(3):
        span = pl.ds(part * width, width)
        for rows, hidden_ref in ((own, hidden_own_ref), (other, hidden_other_ref)):
            product = plain_product(hidden_ref[...], weights_ref[:, span])
            if part != 1:
                product = product + bias_ref[pl.ds(part // 2, 1), :]
            wide[rows, span] = product
    qkv_ref[...] = wide[...].astype(jnp.bfloat16)
    mixed_wide[...] = jnp.zeros_like(mixed_wide)
    lane_low = lax.broadcasted_iota(jnp.int32, (1, LANES), 1) < D // HEADS

    def one_image(image, carry):
        window = pl.ds(pl.multiple_of(image * WINDOW_STEP, 16), WINDOW)
        row_live, column_live = window_masks(image)
        for pair in range(width // LANES):
            query_pair = qkv_ref[window, pl.ds(pair * LANES, LANES)]
            key_pair = qkv_ref[window, pl.ds(width + pair * LANES, LANES)]
            value_pair = qkv_ref[window, pl.ds(2 * width + pair * LANES, LANES)]
            sides = []
            for lane_mask in (lane_low, ~lane_low):
                chances = window_chances(
                    jnp.where(lane_mask, query_pair, jnp.zeros_like(query_pair)),
                    key_pair,
                    row_live,
                    column_live,
                    scale,
                )
                sides.append(plain_product(chances.astype(jnp.bfloat16), value_pair))
            mixed_wide[window, pl.ds(pair * LANES, LANES)] += jnp.where(
                lane_low, sides[0], sides[1]
            )
        return carry

    lax.fori_loop(0, IMG_DEV, one_image, 0)
    turned = weights_ref[:, 3 * width :]
    mixed_own = mixed_wide[own, :].astype(jnp.bfloat16)
    mixed_other = mixed_wide[other, :].astype(jnp.bfloat16)
    mixed_own_ref[...] = mixed_own
    mixed_other_ref[...] = mixed_other
    sent_ref[...] = turned_product(mixed_other, turned).astype(jnp.bfloat16)
    kept_ref[...] = turned_product(mixed_own, turned)


def attend_back_kernel(
    place_ref,
    branch_own_ref,
    branch_other_ref,
    qkv_ref,
    weights_ref,
    stacked_own_ref,
    stacked_other_ref,
    sent_ref,
    kept_ref,
    sums_ref,
    mixed_grad,
    wide,
):
    width = mixed_grad.shape[1]
    row_count = sent_ref.shape[0]
    scale = (D // HEADS) ** (-0.5)
    place = place_ref[0]
    other = pl.ds(pl.multiple_of((1 - place) * row_count, 8), row_count)
    own = pl.ds(pl.multiple_of(place * row_count, 8), row_count)
    turned = weights_ref[:, 3 * width :]
    wide[own, :width] = plain_product(branch_own_ref[...], turned)
    wide[other, :width] = plain_product(branch_other_ref[...], turned)
    mixed_grad[...] = wide[:, :width].astype(jnp.bfloat16)
    wide[...] = jnp.zeros_like(wide)
    lane_low = lax.broadcasted_iota(jnp.int32, (1, LANES), 1) < D // HEADS

    def one_image(image, carry):
        window = pl.ds(pl.multiple_of(image * WINDOW_STEP, 16), WINDOW)
        row_live, column_live = window_masks(image)
        for pair in range(width // LANES):
            query_pair = qkv_ref[window, pl.ds(pair * LANES, LANES)]
            key_pair = qkv_ref[window, pl.ds(width + pair * LANES, LANES)]
            value_pair = qkv_ref[window, pl.ds(2 * width + pair * LANES, LANES)]
            grad_pair = mixed_grad[window, pl.ds(pair * LANES, LANES)]
            sides = []
            for lane_mask in (lane_low, ~lane_low):
                chances = window_chances(
                    jnp.where(lane_mask, query_pair, jnp.zeros_like(query_pair)),
                    key_pair,
                    row_live,
                    column_live,
                    scale,
                )
                weight_grad = turned_product(
                    jnp.where(lane_mask, grad_pair, jnp.zeros_like(grad_pair)), value_pair
                )
                row_sum = jnp.sum(weight_grad * chances, axis=-1, keepdims=True)
                score_grad = (chances * (weight_grad - row_sum)).astype(jnp.bfloat16)
                sides.append(
                    (
                        plain_product(score_grad, key_pair) * scale,
                        row_product(score_grad, query_pair) * scale,
                        row_product(chances.astype(jnp.bfloat16), grad_pair),
                    )
                )
            for part in range(3):
                wide[window, pl.ds(part * width + pair * LANES, LANES)] += jnp.where(
                    lane_low, sides[0][part], sides[1][part]
                )
        return carry

    lax.fori_loop(0, IMG_DEV, one_image, 0)
    weight = weights_ref[:, : 3 * width]
    stacked_own = wide[own, :].astype(jnp.bfloat16)
    stacked_other = wide[other, :].astype(jnp.bfloat16)
    stacked_own_ref[...] = stacked_own
    stacked_other_ref[...] = stacked_other
    sums_ref[...] = jnp.sum(stacked_own.astype(jnp.float32), axis=0, keepdims=True) + jnp.sum(
        stacked_other.astype(jnp.float32), axis=0, keepdims=True
    )
    sent_ref[...] = turned_product(stacked_other, weight).astype(jnp.bfloat16)
    kept_ref[...] = turned_product(stacked_own, weight)


def mlp_kernel(hidden_ref, up_ref, turned_ref, bias_ref, act_ref, slope_ref, partial_ref):
    pre = plain_product(hidden_ref[...], up_ref[...]) + bias_ref[...]
    normal = 0.5 * (1.0 + lax.erf(pre * (0.5**0.5)))
    density = jnp.exp(-0.5 * pre * pre) * (0.5 / math.pi) ** 0.5
    active = (pre * normal).astype(jnp.bfloat16)
    act_ref[...] = active
    slope_ref[...] = (normal + pre * density).astype(jnp.bfloat16)
    partial_ref[...] = turned_product(active, turned_ref[...]).astype(partial_ref.dtype)


def mlp_back_kernel(branch_ref, slope_ref, turned_ref, up_ref, pre_ref, sums_ref, partial_ref):
    act_grad = plain_product(branch_ref[...], turned_ref[...])
    pre_grad = (act_grad * slope_ref[...].astype(jnp.float32)).astype(jnp.bfloat16)
    pre_ref[...] = pre_grad
    sums_ref[...] = jnp.sum(pre_grad.astype(jnp.float32), axis=0, keepdims=True)
    partial_ref[...] = turned_product(pre_grad, up_ref[...]).astype(partial_ref.dtype)


def grads_kernel(*refs):
    first_left, first_right, second_left, second_right = (
        (refs[2 * pair], refs[2 * pair + 1]) for pair in range(4)
    )
    grad_ref = refs[-1]
    cut = first_right[0].shape[1]
    for span, lefts, rights in (
        (slice(0, cut), first_left, first_right),
        (slice(cut, None), second_left, second_right),
    ):
        grad_ref[:, span] = sum(
            row_product(left[...], right[...]) for left, right in zip(lefts, rights)
        ).astype(jnp.bfloat16)


ROOM = 60 * 1024 * 1024


def columns(array, width, place):
    return array, pl.BlockSpec((array.shape[0], width), lambda step: (0, place))


def whole(array):
    return array, pl.BlockSpec(array.shape, lambda step: (0,) * array.ndim)


def scalar(array):
    return array, pl.BlockSpec(memory_space=pltpu.SMEM)


def run_kernel(kernel, operands, results, scratch=(), name=None, flops=0):
    outs = [jax.ShapeDtypeStruct(shape, dtype) for shape, dtype in results]
    return pl.pallas_call(
        kernel,
        grid=(1,),
        in_specs=[spec for array, spec in operands],
        out_specs=[pl.BlockSpec(shape, lambda step, rank=len(shape): (0,) * rank) for shape, dtype in results],
        out_shape=outs,
        scratch_shapes=list(scratch),
        compiler_params=pltpu.CompilerParams(vmem_limit_bytes=ROOM),
        cost_estimate=pl.CostEstimate(
            flops=flops,
            transcendentals=0,
            bytes_accessed=sum(math.prod(out.shape) * out.dtype.itemsize for out in outs),
        ),
        name=name,
    )(*[array for array, spec in operands])


def packed_grads(pairs, total, width, place, held=None):
    operands = [
        (part, pl.BlockSpec((part.shape[0], GRAD_ROWS), lambda step: (0, step)))
        if side % 2 == 0
        else whole(part)
        for side, pair in enumerate(pairs)
        for part in pair
    ]
    aliases = {}
    if held is not None:
        aliases = {len(operands): 0}
        operands.append((held, pl.BlockSpec(memory_space=pl.ANY)))
    return pl.pallas_call(
        grads_kernel,
        grid=(D // GRAD_ROWS,),
        in_specs=[spec for array, spec in operands],
        out_specs=pl.BlockSpec((GRAD_ROWS, width), lambda step: (step, place)),
        out_shape=jax.ShapeDtypeStruct((D, total), jnp.bfloat16),
        input_output_aliases=aliases,
        compiler_params=pltpu.CompilerParams(vmem_limit_bytes=ROOM),
        name="packed_grads",
    )(*[array for array, spec in operands])


def on_device(
    tokens,
    qkv_weight,
    out_weight,
    up_weight,
    down_weight,
    norm_gain,
    norm_shift,
    qv_bias,
    out_bias,
    up_bias,
    cotangent,
):
    tp_index = lax.axis_index("tp")
    tp_count = lax.axis_size("tp")
    fsdp_count = lax.axis_size("fsdp")
    row_count = tokens.shape[0]
    local_width = qkv_weight.shape[3]
    inner_width = up_weight.shape[2]
    piece_rows = qkv_weight.shape[1]
    all_rows = IMG_DEV * SEQ
    slot_rows = row_count * tp_count
    live = (tp_index * row_count + jnp.arange(row_count) < all_rows)[:, None]
    cut_qkv = 3 * local_width
    cut_out = cut_qkv + local_width

    place = jnp.reshape(tp_index, (1,)).astype(jnp.int32)
    bf16 = jnp.bfloat16
    f32 = jnp.float32

    def attn_pieces(layer_index):
        return [
            qkv_weight[layer_index].reshape(piece_rows, cut_qkv),
            out_weight[layer_index].T,
        ]

    def mlp_pieces(layer_index):
        return [up_weight[layer_index], down_weight[layer_index].T]

    joint = 2 * inner_width + cut_out
    sources = []
    for layer_index in range(LAYERS):
        full = gathered(mlp_pieces(layer_index) + attn_pieces(layer_index))
        sources.append(
            (columns(full, cut_out, 2), columns(full, inner_width, 0), columns(full, inner_width, 1))
        )

    def back_half(branch, slope, down_side, up_side, kind):
        pre_grad, sums, partial_sum = run_kernel(
            mlp_back_kernel,
            [whole(branch), whole(slope), down_side, up_side],
            [((row_count, inner_width), bf16), ((1, inner_width), f32), ((row_count, D), kind)],
            name="mlp_back",
        )
        return pre_grad, partial_sum, sums

    grad = jnp.where(live, cotangent.astype(f32), 0.0)
    branch_own = grad.astype(bf16)
    stream = tokens.astype(jnp.float32)
    saved_values = []
    for layer_index in range(LAYERS):
        attn_side, up_side, down_side = sources[layer_index]
        local_qv = lax.dynamic_slice_in_dim(
            qv_bias[layer_index], tp_index * local_width, local_width, 1
        )
        local_up = lax.dynamic_slice_in_dim(
            up_bias[layer_index], tp_index * inner_width, inner_width, 0
        )[None]
        layer_input = stream
        own_hidden = norm_rows(
            stream, norm_gain[layer_index, 0], norm_shift[layer_index, 0]
        ).astype(bf16)
        other_hidden = swap(own_hidden)
        qkv, mixed_own, mixed_other, sent, kept = run_kernel(
            attend_kernel,
            [scalar(place), whole(own_hidden), whole(other_hidden), attn_side, whole(local_qv)],
            [
                ((slot_rows, cut_qkv), bf16),
                ((row_count, local_width), bf16),
                ((row_count, local_width), bf16),
                ((row_count, D), bf16),
                ((row_count, D), f32),
            ],
            [pltpu.VMEM((slot_rows, local_width), f32), pltpu.VMEM((slot_rows, cut_qkv), f32)],
            name="attend",
        )
        stream = stream + (kept + swap(sent).astype(f32)) + out_bias[layer_index, 0]
        middle = stream
        hidden_own = norm_rows(
            stream, norm_gain[layer_index, 1], norm_shift[layer_index, 1]
        ).astype(bf16)
        hidden_other = swap(hidden_own)

        def mlp_half(hidden_half, kind):
            return run_kernel(
                mlp_kernel,
                [whole(hidden_half), up_side, down_side, whole(local_up)],
                [
                    ((row_count, inner_width), bf16),
                    ((row_count, inner_width), bf16),
                    ((row_count, D), kind),
                ],
                name="mlp",
            )

        act_own, slope_own, kept = mlp_half(hidden_own, f32)
        if layer_index < LAYERS - 1:
            hidden_other, kept = lax.optimization_barrier((hidden_other, kept))
        else:
            pre_own, kept_back, up_sums_own = back_half(
                branch_own, slope_own, down_side, up_side, f32
            )
            hidden_other, kept, kept_back = lax.optimization_barrier(
                (hidden_other, kept, kept_back)
            )
        act_other, slope_other, sent = mlp_half(hidden_other, bf16)
        if layer_index < LAYERS - 1:
            stream = stream + (kept + swap(sent).astype(f32)) + out_bias[layer_index, 1]
        else:
            last_sent, last_kept = sent, kept
        saved_values.append(
            (
                layer_input,
                middle,
                (own_hidden, other_hidden),
                qkv,
                (mixed_own, mixed_other),
                hidden_own,
                hidden_other,
                slope_own,
                slope_other,
                act_own,
                act_other,
                (attn_side, up_side, down_side),
            )
        )
    held = None
    scattered_grads = []
    gain_grads = [None] * LAYERS
    shift_grads = [None] * LAYERS
    qv_grads = [None] * LAYERS
    out_bias_grads = [None] * LAYERS
    up_bias_grads = [None] * LAYERS
    for layer_index in reversed(range(LAYERS)):
        (
            layer_input,
            middle,
            hidden_pair,
            qkv,
            mixed_pair,
            hidden_own,
            hidden_other,
            slope_own,
            slope_other,
            act_own,
            act_other,
            (attn_side, up_side, down_side),
        ) = saved_values[layer_index]
        branch_other = swap(branch_own)
        down_bias_grad = jnp.sum(branch_own.astype(f32), axis=0)
        if layer_index < LAYERS - 1:
            pre_own, kept_back, up_sums_own = back_half(
                branch_own, slope_own, down_side, up_side, f32
            )
            branch_other, kept_back = lax.optimization_barrier((branch_other, kept_back))
        pre_other, sent, up_sums_other = back_half(
            branch_other, slope_other, down_side, up_side, bf16
        )
        up_vector_grad = (up_sums_own + up_sums_other)[0]
        mlp_grad = packed_grads(
            [
                (hidden_own, hidden_other),
                (pre_own, pre_other),
                (branch_own, branch_other),
                (act_own, act_other),
            ],
            2 * inner_width if held is None else joint,
            2 * inner_width,
            0,
            held,
        )
        received, mlp_grad = lax.optimization_barrier((swap(sent), mlp_grad))
        norm_grad = kept_back + received.astype(f32)
        scattered_grads.append(scattered(mlp_grad))
        norm_back = jax.vjp(
            norm_rows, middle, norm_gain[layer_index, 1], norm_shift[layer_index, 1]
        )[1]
        middle_grad, gain_two, shift_two = norm_back(norm_grad)
        grad = grad + middle_grad
        branch_own = grad.astype(bf16)
        attn_bias_grad = jnp.sum(branch_own.astype(f32), axis=0)
        branch_other = swap(branch_own)
        if layer_index == LAYERS - 1:
            branch_other, last_sent = lax.optimization_barrier((branch_other, last_sent))
            last_received = swap(last_sent)
        stacked_own, stacked_other, sent, kept, stacked_sums = run_kernel(
            attend_back_kernel,
            [scalar(place), whole(branch_own), whole(branch_other), whole(qkv), attn_side],
            [
                ((row_count, cut_qkv), bf16),
                ((row_count, cut_qkv), bf16),
                ((row_count, D), bf16),
                ((row_count, D), f32),
                ((1, cut_qkv), f32),
            ],
            [pltpu.VMEM((slot_rows, local_width), bf16), pltpu.VMEM((slot_rows, cut_qkv), f32)],
            name="attend_back",
        )
        stacked_sums = stacked_sums.reshape(3, local_width)
        attn_grad = packed_grads(
            [hidden_pair, (stacked_own, stacked_other), (branch_own, branch_other), mixed_pair],
            joint if layer_index else cut_out,
            cut_out,
            2 if layer_index else 0,
        )
        if layer_index == LAYERS - 1:
            sent, last_received = lax.optimization_barrier((sent, last_received))
            stream = stream + (last_kept + last_received.astype(f32)) + out_bias[layer_index, 1]
            activations = jnp.where(live, stream, 0.0).astype(bf16)
        received, attn_grad = lax.optimization_barrier((swap(sent), attn_grad))
        norm_grad = kept + received.astype(f32)
        held = attn_grad
        norm_back = jax.vjp(
            norm_rows, layer_input, norm_gain[layer_index, 0], norm_shift[layer_index, 0]
        )[1]
        input_part, gain_one, shift_one = norm_back(norm_grad)
        grad = grad + input_part
        branch_own = grad.astype(bf16)
        gain_grads[layer_index] = jnp.stack([gain_one, gain_two])
        shift_grads[layer_index] = jnp.stack([shift_one, shift_two])
        qv_local = jnp.stack([stacked_sums[0], stacked_sums[2]])
        qv_grads[layer_index] = lax.dynamic_update_slice_in_dim(
            jnp.zeros((2, D), jnp.float32), qv_local, tp_index * local_width, 1
        )
        out_bias_grads[layer_index] = jnp.stack([attn_bias_grad, down_bias_grad])
        up_bias_grads[layer_index] = lax.dynamic_update_slice_in_dim(
            jnp.zeros((FF,), jnp.float32), up_vector_grad, tp_index * inner_width, 0
        ).reshape(FF // D, D)
    small = jnp.concatenate(
        gain_grads + shift_grads + qv_grads + out_bias_grads + up_bias_grads, axis=0
    )
    attn_first, small = reduced_together(held, small, fsdp_count)
    pair = 2 * LAYERS
    small_totals = [small[pair * k : pair * (k + 1)].reshape(LAYERS, 2, D) for k in range(4)]
    up_totals = small[4 * pair :].reshape(LAYERS, FF)
    mlp_last, joint_owned = scattered_grads
    owned = [
        (joint_owned[:, : 2 * inner_width], attn_first),
        (mlp_last, joint_owned[:, 2 * inner_width :]),
    ]
    up_all = jnp.stack([mlp[:, :inner_width] for mlp, attn in owned])
    down_all = jnp.stack([mlp[:, inner_width:].T for mlp, attn in owned])
    qkv_all = jnp.stack(
        [attn[:, :cut_qkv].reshape(piece_rows, 3, local_width) for mlp, attn in owned]
    )
    out_all = jnp.stack([attn[:, cut_qkv:].T for mlp, attn in owned])
    input_grad = jnp.where(live, grad, 0.0)
    return (
        activations,
        input_grad,
        qkv_all,
        out_all,
        up_all,
        down_all,
        small_totals[0],
        small_totals[1],
        small_totals[2],
        small_totals[3],
        up_totals,
    )


def solution(mesh):
    return jax.shard_map(
        on_device,
        mesh=mesh,
        in_specs=(
            P(("fsdp", "tp"), None),
            P(None, "fsdp", None, "tp"),
            P(None, "tp", "fsdp"),
            P(None, "fsdp", "tp"),
            P(None, "tp", "fsdp"),
            P(),
            P(),
            P(),
            P(),
            P(),
            P(("fsdp", "tp"), None),
        ),
        out_specs=(
            P(("fsdp", "tp"), None),
            P(("fsdp", "tp"), None),
            P(None, "fsdp", None, "tp"),
            P(None, "tp", "fsdp"),
            P(None, "fsdp", "tp"),
            P(None, "tp", "fsdp"),
            P(),
            P(),
            P(),
            P(),
            P(),
        ),
        check_vma=False,
    )
```
